32 devices in a mesh: shard: 2 (over y), rep: 16 (over z, x, core).
Axes of the slice: x: 2, y: 2, z: 4, core: 2. Of those that a mesh axis runs over, the one named last changes fastest.
Arguments:
- layer_in: bfloat16 [32768, 768], P(('shard', 'rep')), may hold values from -6 to 6
- segment_ids: int32 [32, 1024], P(('shard', 'rep')), may hold values from 0 to 2, never falling along the last dimension, each value on 1 to 512 neighbouring positions
- cotangent: bfloat16 [32768, 768], P(('shard', 'rep')), may hold values from -6 to 6
- norm_gain: bfloat16 [768], P('shard'), may hold values from 0.5 to 1.5
- in_weight: bfloat16 [768, 3352], P('shard'), may hold values from -0.21875 to 0.21875
- conv_weight: bfloat16 [4, 1792], P(None, 'shard'), may hold values from -3 to 3
- conv_bias: bfloat16 [1792], P('shard'), may hold values from -0.5 to 0.5
- dt_bias: bfloat16 [24], P('shard'), may hold values from -7 to -3
- a_log: bfloat16 [24], P('shard'), may hold values from 0 to 2.765625
- skip_gain: bfloat16 [24], P('shard'), may hold values from 0.5 to 1.5
- gate_gain: bfloat16 [1536], P('shard'), may hold values from 0.5 to 1.5
- out_weight: bfloat16 [1536, 768], P('shard'), may hold values from -0.15625 to 0.15625
Outputs:
- layer_out: bfloat16 [32768, 768], P(('shard', 'rep'))
- input_grad: bfloat16 [32768, 768], P(('shard', 'rep'))
- norm_gain_grad: float32 [768], P('shard')
- in_weight_grad: float32 [768, 3352], P('shard')
- conv_weight_grad: float32 [4, 1792], P(None, 'shard')
- conv_bias_grad: float32 [1792], P('shard')
- dt_bias_grad: float32 [24], P('shard')
- a_log_grad: float32 [24], P('shard')
- skip_grad: float32 [24], P('shard')
- gate_gain_grad: float32 [1536], P('shard')
- out_weight_grad: float32 [1536, 768], P('shard')
The draws below stay inside these ranges and needn't reach their ends.
Inputs may be any that keep to these rules, and one draw needn't show every extreme that they name: `segment_ids`: within each row the numbers never fall; a document spans 1 to 512 tokens and some document in each row spans exactly that.
All inputs are finite; a program needn't handle non-finite values.
Results may differ from the reference program's by a relative error of at most 0.012.
Values may be sent and summed in bfloat16 or wider, within the bound.
A program may use at most 192 MiB of HBM per device.

```python
import math
import jax
import jax.numpy as jnp
import numpy as np
from jax import lax

D = 768
HEADS = 24
HEADDIM = 64
STATE = 128
CONV = 4
STRETCH = 256
TOK_DEV = 1024
INNER = 1536
XBC = 1792
PROJ = 3352
NSEQ = 32
TOKENS = 32768


def level_of(own_key, extent, shards, low, top_value):
    loudness = 1.0
    for axis_at, shards_of in shards:
        heights = jax.random.uniform(jax.random.fold_in(jax.random.fold_in(own_key, 6), axis_at), (shards_of,), jnp.float32, low / len(shards), top_value / len(shards))
        loudness = loudness * jnp.repeat(jnp.exp(heights), extent[axis_at] // shards_of).reshape((-1,) + (1,) * (len(extent) - 1 - axis_at))
    return loudness


def length_profile(amount, total, most, skew):
    portions = [(1 << 20) // math.isqrt(rank ** skew) + 1 for rank in range(2, amount + 1)]
    surplus, given = total - most - (amount - 1), [1] * (amount - 1)
    while surplus > 0:
        candidates = [i for i in range(amount - 1) if given[i] < most]
        mass, budget = sum([portions[i] for i in candidates]), surplus
        for i in candidates:
            extra = min(most - given[i], max(1, budget * portions[i] // mass), surplus)
            given[i] = given[i] + extra
            surplus = surplus - extra
    return np.array([most] + given)


def ragged_sizes(own_key, amount, total, bound, slope):
    if amount == 2:
        one = jax.random.randint(own_key, (), max(1, total - bound), min(bound, total - 1) + 1)
        return jnp.stack([one, total - one])
    tallies = jnp.asarray(length_profile(amount, total, bound, slope), jnp.int32)
    twos = (amount - 1) // 2
    giver, taker = tallies[1:1 + 2 * twos:2], tallies[2:2 + 2 * twos:2]
    room = jnp.minimum(giver - 1, bound - taker)
    moved = jax.random.randint(jax.random.fold_in(own_key, 1), (twos,), 0, 1 << 20) % (room + 1)
    tallies = tallies.at[1:1 + 2 * twos:2].set(giver - moved).at[2:2 + 2 * twos:2].set(taker + moved)
    return tallies[jax.random.permutation(jax.random.fold_in(own_key, 2), amount)]


def centred(own_key, shape, width, bound, split=(), dtype=jnp.bfloat16):
    values = width * jax.random.normal(own_key, shape, jnp.float32)
    if split:
        values = values * level_of(own_key, shape, split, -0.22, 0.18)
    return jnp.clip(values, -bound, bound).astype(dtype)


def setup_inputs(seed: int = 0) -> dict:
    key_list = jax.random.split(jax.random.key(seed), 13)
    layer_in = centred(key_list[0], (TOKENS, D), 1.0, 6.0, ((0, 32),))
    segment_ids = jax.vmap(lambda own: jnp.searchsorted(jnp.cumsum(ragged_sizes(own, max(3, TOK_DEV // 512), TOK_DEV, TOK_DEV // 2, 1)), jnp.arange(TOK_DEV), side="right"))(jax.random.split(key_list[1], NSEQ)).reshape((NSEQ, TOK_DEV)).astype(jnp.int32)
    cotangent = centred(key_list[2], (TOKENS, D), 1.0, 6.0, ((0, 32),))
    norm_gain = jnp.clip(1.0 + 0.1 * jax.random.normal(key_list[3], (D,), jnp.float32), 0.5, 1.5).astype(jnp.bfloat16)
    in_weight = centred(key_list[4], (D, PROJ), D ** -0.5, 0.21875, ((0, 2),))
    conv_weight = centred(key_list[5], (CONV, XBC), CONV ** -0.5, 3.0, ((1, 2),))
    conv_bias = jnp.clip(jax.random.uniform(key_list[6], (XBC,), jnp.float32, -0.5, 0.5) * level_of(key_list[6], (XBC,), ((0, 2),), -0.4, 0.0), -0.5, 0.5).astype(jnp.bfloat16)
    dt_bias = jnp.clip(-7.0 + 4.0 * jax.random.uniform(key_list[7], (HEADS,), jnp.float32) ** level_of(key_list[7], (HEADS,), ((0, 2),), -0.2, 0.2), -7.0, -3.0).astype(jnp.bfloat16)
    a_log = jnp.clip(2.765625 * jax.random.uniform(key_list[8], (HEADS,), jnp.float32) ** level_of(key_list[8], (HEADS,), ((0, 2),), -0.2, 0.2), 0.0, 2.765625).astype(jnp.bfloat16)
    skip_gain = jnp.clip(0.5 + 1.0 * jax.random.uniform(key_list[9], (HEADS,), jnp.float32) ** level_of(key_list[9], (HEADS,), ((0, 2),), -0.2, 0.2), 0.5, 1.5).astype(jnp.bfloat16)
    gate_gain = jnp.clip(1.0 + 0.1 * jax.random.normal(key_list[10], (INNER,), jnp.float32), 0.5, 1.5).astype(jnp.bfloat16)
    out_weight = centred(key_list[11], (INNER, D), INNER ** -0.5, 0.15625, ((0, 2),))
    return {"layer_in": layer_in, "segment_ids": segment_ids, "cotangent": cotangent, "norm_gain": norm_gain, "in_weight": in_weight, "conv_weight": conv_weight, "conv_bias": conv_bias, "dt_bias": dt_bias, "a_log": a_log, "skip_gain": skip_gain, "gate_gain": gate_gain, "out_weight": out_weight}


eps = 1e-05
highest = lax.Precision.HIGHEST

@jax.custom_vjp
def low(v):
    return lax.optimization_barrier(v.astype(jnp.bfloat16)).astype(jnp.float32)

@jax.custom_vjp
def low_back(v):
    return v

def low_keep(v):
    return (low(v), None)

def low_pass(kept, grad):
    return (grad,)

def back_keep(v):
    return (v, None)

def back_low(kept, grad):
    return (low(grad),)
low.defvjp(low_keep, low_pass)
low_back.defvjp(back_keep, back_low)

def block_step(carry_in, inputs):
    hidden, last_segment = carry_in
    values_flat, b_rows, c_rows, step_t, decay_t, segment = inputs
    length = segment.shape[0]
    values = values_flat.reshape(length, HEADS, HEADDIM)
    running_t = jnp.cumsum(decay_t, axis=1)
    position = jnp.arange(length)
    allowed = (position[:, None] >= position[None, :]) & (segment[:, None] == segment[None, :])
    spread_log = jnp.where(allowed[None], running_t[:, :, None] - running_t[:, None, :], -1e+30)
    kernel = jnp.exp(spread_log)
    pair_scores = jnp.dot(c_rows, b_rows.T, precision=highest)
    weighted = values * step_t.T[:, :, None]
    local_part = jnp.einsum('hts,shp->thp', kernel * pair_scores[None], weighted, precision=highest)
    keep_in = (segment == last_segment).astype(jnp.float32)
    entering = jnp.exp(running_t) * keep_in[None, :]
    carried_part = jnp.einsum('tn,hpn->thp', c_rows, hidden, precision=highest) * entering.T[:, :, None]
    keep_end = (segment == segment[-1]).astype(jnp.float32)
    leaving = jnp.exp(running_t[:, -1:] - running_t) * keep_end[None, :]
    carried = jnp.exp(running_t[:, -1]) * (segment[-1] == last_segment).astype(jnp.float32)
    new_state = hidden * carried[:, None, None] + jnp.einsum('shp,sn->hpn', weighted * leaving.T[:, :, None], b_rows, precision=highest)
    return ((new_state, segment[-1]), (local_part + carried_part).reshape(length, HEADS * HEADDIM))

def state_scan(values, b_rows, c_rows, step_sizes, decay_log, segment):
    length = segment.shape[0]
    blocks = length // STRETCH
    inputs = (values.reshape(blocks, STRETCH, HEADS * HEADDIM), b_rows.reshape(blocks, STRETCH, STATE), c_rows.reshape(blocks, STRETCH, STATE), jnp.transpose(step_sizes.reshape(blocks, STRETCH, HEADS), (0, 2, 1)), jnp.transpose(decay_log.reshape(blocks, STRETCH, HEADS), (0, 2, 1)), segment.reshape(blocks, STRETCH))
    start = (jnp.zeros((HEADS, HEADDIM, STATE), jnp.float32), jnp.array(-1, jnp.int32))
    ending, outputs = lax.scan(jax.checkpoint(block_step), start, inputs)
    return outputs.reshape(length, HEADS, HEADDIM)

def middle(projected, conv_w, conv_b, step_bias, alog, skip, gate_vec, segment):
    length = segment.shape[0]
    gate_part = projected[:, :INNER]
    conv_input = projected[:, INNER:INNER + XBC]
    raw_step = projected[:, INNER + XBC:]
    convolved = jnp.zeros((length, XBC), jnp.float32) + conv_b[None, :]
    for offset in range(CONV):
        shifted = jnp.pad(conv_input, ((offset, 0), (0, 0)))[:length]
        shifted_seg = jnp.pad(segment, (offset, 0), constant_values=-1)[:length]
        same_doc = (shifted_seg == segment).astype(jnp.float32)
        convolved = convolved + conv_w[CONV - 1 - offset][None, :] * shifted * same_doc[:, None]
    active = jax.nn.silu(convolved)
    values = active[:, :INNER].reshape(length, HEADS, HEADDIM)
    b_rows = active[:, INNER:INNER + STATE]
    c_rows = active[:, INNER + STATE:]
    step_sizes = jax.nn.softplus(raw_step + step_bias[None, :])
    decay_log = -jnp.exp(alog)[None, :] * step_sizes
    outputs = state_scan(values, b_rows, c_rows, step_sizes, decay_log, segment) + skip[None, :, None] * values
    gated = outputs.reshape(length, INNER) * jax.nn.silu(gate_part)
    inv_rms = lax.rsqrt(lax.optimization_barrier(jnp.mean(gated * gated, axis=-1, keepdims=True)) + eps)
    return gated * inv_rms * gate_vec[None, :]

def normalize(features, gain_vec):
    inv_rms = lax.rsqrt(lax.optimization_barrier(jnp.mean(features * features, axis=-1, keepdims=True)) + eps)
    return features * inv_rms * gain_vec[None, :]

def whole_layer(features, gain_vec, in_w, conv_w, conv_b, step_bias, alog, skip, gate_vec, out_w, segment):
    normed = low(normalize(features, gain_vec))
    projected = low_back(jnp.dot(normed, in_w, precision=highest))
    mixed = low(middle(projected, conv_w, conv_b, step_bias, alog, skip, gate_vec, segment))
    return features + jnp.dot(mixed, out_w, precision=highest)

def reference(layer_in, segment_ids, cotangent, norm_gain, in_weight, conv_weight, conv_bias, dt_bias, a_log, skip_gain, gate_gain, out_weight):
    params = tuple((p.astype(jnp.float32) for p in (norm_gain, in_weight, conv_weight, conv_bias, dt_bias, a_log, skip_gain, gate_gain, out_weight)))
    inputs = (layer_in.astype(jnp.float32).reshape(NSEQ, TOK_DEV, D), segment_ids, cotangent.astype(jnp.float32).reshape(NSEQ, TOK_DEV, D))

    def per_sequence(totals, sequence):
        features, segment, grad_out = sequence

        def applied(feature_in, *weights):
            return whole_layer(feature_in, *weights, segment)
        result, pullback = jax.vjp(applied, features, *params)
        gradients = pullback(grad_out)
        totals = tuple((a + b for a, b in zip(totals, gradients[1:])))
        return (totals, (result.astype(jnp.bfloat16), gradients[0].astype(jnp.bfloat16)))
    zeros = tuple((jnp.zeros_like(p) for p in params))
    totals, (results, feature_grads) = lax.scan(per_sequence, zeros, inputs)
    averaged = tuple((t / NSEQ for t in totals))
    return (results.reshape(TOKENS, D), feature_grads.reshape(TOKENS, D), averaged[0], averaged[1], averaged[2], averaged[3], averaged[4], averaged[5], averaged[6], averaged[7], averaged[8])
```

```python
import functools

import jax
import jax.numpy as jnp
from jax import lax
from jax.experimental import pallas as pl
from jax.experimental.pallas import tpu as pltpu
from jax.sharding import PartitionSpec as P

HEADS = 24
HEADDIM = 64
STATE = 128
CONV = 4
BLOCK = 128
INNER = 1536
XBC = 1792
WIDE = INNER + XBC
LANES = 128

MESH = pl.DeviceIdType.MESH
eps = 1e-05
highest = lax.Precision.HIGHEST
f32 = jnp.float32
bf16 = jnp.bfloat16


def mm(a, b, contract=((1,), (0,))):
    return lax.dot_general(a, b, (contract, ((), ())), preferred_element_type=f32)


def mm_t(a, w_ref, start, stop):
    half = w_ref.shape[2]
    nt = ((1,), (1,))
    return mm(a[:, :half], w_ref[0, start:stop], nt) + mm(a[:, half:], w_ref[1, start:stop], nt)


def sigmoid(v):
    return 1.0 / (1.0 + jnp.exp(-v))


def softplus(v):
    small = jnp.exp(-jnp.abs(v))
    series = small * (1.0 - small * (0.5 - small * (1.0 / 3.0 - small * 0.25)))
    return jnp.maximum(v, 0.0) + jnp.where(small < 0.03, series, jnp.log(1.0 + small))


def spread(per_head, spread_mat):
    high = per_head.astype(bf16)
    rest = (per_head - high.astype(f32)).astype(bf16)
    return mm(jnp.concatenate([high, rest], axis=1), spread_mat)


def head_sum(per_channel, spread_mat):
    high = per_channel.astype(bf16)
    rest = (per_channel - high.astype(f32)).astype(bf16)
    one = spread_mat[:LANES, :]
    return mm(high, one, ((1,), (1,))) + mm(rest, one, ((1,), (1,)))


def block_terms(raw, aux, seg_row, head_vecs):
    length = raw.shape[0]
    pre = raw + head_vecs[0:1, :]
    step = softplus(pre)
    rate = -jnp.exp(head_vecs[1:2, :])
    decay = rate * step
    row = lax.broadcasted_iota(jnp.int32, (length, length), 0)
    col = lax.broadcasted_iota(jnp.int32, (length, length), 1)
    lower = (row >= col).astype(f32)
    running = lax.dot_general(
        lower, decay, (((1,), (0,)), ((), ())), precision=highest, preferred_element_type=f32
    )
    allowed = (row >= col) & (aux[:, 5:6] == seg_row)
    entering = jnp.exp(running) * aux[:, 3:4]
    leaving = jnp.exp(running[length - 1 : length, :] - running) * aux[:, 4:5]
    return pre, step, rate, decay, running, allowed, entering, leaving, lower


def lane_pair(values, first):
    lane = lax.broadcasted_iota(jnp.int32, values.shape, 1)
    zero = jnp.zeros_like(values)
    return jnp.concatenate(
        [jnp.where(lane < HEADDIM, values, zero), jnp.where(lane >= HEADDIM, values, zero)], axis=0
    )


def spread_of(running, running_t, head):
    diff = running[:, head : head + 1] - running_t[head : head + 1, :]
    return jnp.exp(jnp.minimum(diff, 0.0))


def forward_kernel(
    u_ref, aux_ref, seg_ref, gain_ref, in_ref, step_ref, conv_w_ref, conv_b_ref, head_ref, skip_ref,
    gate_gain_ref, out_w_ref, spread_ref,
    normed_ref, gate_ref, ci_ref, conv_ref, raw_ref, y_ref, state_ref, mixed_ref, out_ref,
    buf, hidden, y_buf,
):
    @pl.when(pl.program_id(0) == 0)
    def _():
        buf[0:8, :] = jnp.zeros((8, XBC), f32)
        hidden[...] = jnp.zeros_like(hidden)

    u = u_ref[...].astype(f32)
    inv = lax.rsqrt(jnp.mean(u * u, axis=-1, keepdims=True) + eps)
    normed = (u * inv * gain_ref[...]).astype(bf16)
    normed_ref[...] = normed
    gate = mm_t(normed, in_ref, 0, INNER)
    gate_ref[...] = gate
    conv_in = mm_t(normed, in_ref, INNER, WIDE)
    raw = mm(normed, step_ref[...], ((1,), (1,)))
    raw_ref[...] = raw
    ci_ref[...] = conv_in.astype(bf16)
    aux = aux_ref[...]
    buf[8 : 8 + BLOCK, :] = conv_in
    conv = conv_b_ref[...] + conv_w_ref[3:4, :] * conv_in
    for k in range(1, CONV):
        conv = conv + conv_w_ref[3 - k : 4 - k, :] * buf[8 - k : 8 - k + BLOCK, :] * aux[:, k - 1 : k]
    buf[0:8, :] = conv_in[BLOCK - 8 :, :]
    conv_ref[...] = conv
    active = conv * sigmoid(conv)
    values = active[:, :INNER]
    b_low = active[:, INNER : INNER + STATE].astype(bf16)
    c_low = active[:, INNER + STATE :].astype(bf16)
    _, step, _, _, running, allowed, entering, leaving, _ = block_terms(
        raw, aux, seg_ref[0], head_ref[...]
    )
    running_t = jnp.transpose(running)
    spread_mat = spread_ref[...]
    weighted = values * spread(step, spread_mat)
    w_low = weighted.astype(bf16)
    scores = jnp.where(allowed, mm(c_low, b_low, ((1,), (1,))), 0.0)
    enter_wide = spread(entering, spread_mat)
    leave_wide = spread(leaving, spread_mat)
    for pair in range(HEADS // 2):
        cols = slice(pair * LANES, (pair + 1) * LANES)
        first = (spread_of(running, running_t, 2 * pair) * scores).astype(bf16)
        second = (spread_of(running, running_t, 2 * pair + 1) * scores).astype(bf16)
        y_buf[:, cols] = mm(
            jnp.concatenate([first, second], axis=1), lane_pair(w_low[:, cols], pair)
        )
    state = hidden[...]
    state_low = state.astype(bf16)
    state_ref[0] = state_low
    y = y_buf[...] + mm(c_low, state_low) * enter_wide + skip_ref[...] * values
    hidden[...] = state * enter_wide[BLOCK - 1 :, :] + mm(
        b_low, (weighted * leave_wide).astype(bf16), ((0,), (0,))
    )
    y_ref[...] = y
    gated = y * (gate * sigmoid(gate))
    inv_g = lax.rsqrt(jnp.mean(gated * gated, axis=-1, keepdims=True) + eps)
    mixed = (gated * inv_g * gate_gain_ref[...]).astype(bf16)
    mixed_ref[...] = mixed
    out_ref[...] = (u + mm(mixed, out_w_ref[...])).astype(bf16)


def backward_kernel(
    u_ref, g_ref, aux_ref, seg_ref, gain_ref, in_ref, step_ref, conv_w_ref, head_ref, skip_ref,
    gate_gain_ref, out_w_ref, spread_ref, gate_ref, ci_ref, conv_ref, raw_ref, y_ref, state_ref,
    ingrad_ref, zx_ref, rawg_ref, dgain_ref, dconv_w_ref, dconv_b_ref, dhead_ref, dskip_ref,
    dgate_gain_ref,
    buf, d_hidden, dw_buf,
):
    @pl.when(pl.program_id(0) == 0)
    def _():
        buf[BLOCK:, :] = jnp.zeros((8, XBC), f32)
        d_hidden[...] = jnp.zeros_like(d_hidden)
        for ref in (dgain_ref, dconv_w_ref, dconv_b_ref, dhead_ref, dskip_ref, dgate_gain_ref):
            ref[...] = jnp.zeros_like(ref)

    def total(v):
        return jnp.sum(v, axis=0, keepdims=True)

    g = g_ref[...]
    aux = aux_ref[...]
    spread_mat = spread_ref[...]
    mixed_grad = mm(g, out_w_ref[...], ((1,), (1,)))
    gate = gate_ref[...]
    y = y_ref[...]
    gate_sig = sigmoid(gate)
    gate_act = gate * gate_sig
    gated = y * gate_act
    inv_g = lax.rsqrt(jnp.mean(gated * gated, axis=-1, keepdims=True) + eps)
    dgate_gain_ref[...] += total(mixed_grad * gated * inv_g)
    scaled = mixed_grad * gate_gain_ref[...]
    mean_term = jnp.mean(scaled * gated, axis=-1, keepdims=True)
    d_gated = inv_g * scaled - gated * (inv_g * inv_g * inv_g * mean_term)
    dy = d_gated * gate_act
    zx_ref[:, :INNER] = (d_gated * y * (gate_sig * (1.0 + gate * (1.0 - gate_sig)))).astype(bf16)

    conv = conv_ref[...]
    conv_sig = sigmoid(conv)
    active = conv * conv_sig
    slope = conv_sig * (1.0 + conv * (1.0 - conv_sig))
    values = active[:, :INNER]
    b_low = active[:, INNER : INNER + STATE].astype(bf16)
    c_low = active[:, INNER + STATE :].astype(bf16)
    pre, step, rate, decay, running, allowed, entering, leaving, lower = block_terms(
        raw_ref[...], aux, seg_ref[0], head_ref[...]
    )
    running_t = jnp.transpose(running)
    step_wide = spread(step, spread_mat)
    weighted = values * step_wide
    w_low = weighted.astype(bf16)
    scores = jnp.where(allowed, mm(c_low, b_low, ((1,), (1,))), 0.0)
    enter_wide = spread(entering, spread_mat)
    leave_wide = spread(leaving, spread_mat)
    dskip_ref[...] += total(dy * values)
    dy_low = dy.astype(bf16)
    d_scores = jnp.zeros((BLOCK, BLOCK), f32)
    d_running = jnp.zeros((BLOCK, LANES), f32)
    half = lax.broadcasted_iota(jnp.int32, (2 * BLOCK, LANES), 0) // BLOCK
    lane = lax.broadcasted_iota(jnp.int32, (2 * BLOCK, LANES), 1)
    for pair in range(HEADS // 2):
        cols = slice(pair * LANES, (pair + 1) * LANES)
        dy_two = lane_pair(dy_low[:, cols], pair)
        d_kernel = mm(dy_two, w_low[:, cols], ((1,), (1,)))
        spread_a = spread_of(running, running_t, 2 * pair)
        spread_b = spread_of(running, running_t, 2 * pair + 1)
        part_a = d_kernel[:BLOCK] * spread_a
        part_b = d_kernel[BLOCK:] * spread_b
        d_scores = d_scores + (part_a + part_b)
        kernel_two = jnp.concatenate(
            [(spread_a * scores).astype(bf16), (spread_b * scores).astype(bf16)], axis=0
        )
        dw_buf[:, cols] = mm(kernel_two, dy_two, ((0,), (0,)))
        flow_a = (part_a * scores).astype(bf16)
        flow_b = (part_b * scores).astype(bf16)
        marks = jnp.where(lane == 2 * pair + half, 1.0, 0.0).astype(bf16)
        d_running = d_running + (
            mm(jnp.concatenate([flow_a, flow_b], axis=1), marks)
            - mm(jnp.concatenate([flow_a, flow_b], axis=0), marks, ((0,), (0,)))
        )
    state_low = state_ref[0]
    d_state = d_hidden[...]
    d_state_low = d_state.astype(bf16)
    entered = dy * enter_wide
    entered_low = entered.astype(bf16)
    d_running = d_running + head_sum(entered * mm(c_low, state_low), spread_mat)
    left = weighted * leave_wide
    left_low = left.astype(bf16)
    d_left = mm(b_low, d_state_low)
    left_flow = head_sum(left * d_left, spread_mat)
    d_running = d_running - left_flow
    carried = enter_wide[BLOCK - 1 :, :]
    carry_row = total(d_state * state_low.astype(f32)) * carried
    carry_flow = head_sum(jnp.broadcast_to(carry_row, (8, INNER)), spread_mat)[0:1, :]
    d_hidden[...] = d_state * carried + mm(c_low, entered_low, ((0,), (0,)))
    d_weighted = dw_buf[...] + d_left * leave_wide
    d_decay = (
        lax.dot_general(
            lower, d_running, (((0,), (0,)), ((), ())), precision=highest, preferred_element_type=f32
        )
        + total(left_flow)
        + carry_flow
    )
    d_step = d_decay * rate + head_sum(d_weighted * values, spread_mat)
    d_raw = d_step * sigmoid(pre)
    dhead_ref[0:1, :] += total(d_raw)
    dhead_ref[1:2, :] += total(d_decay * decay)
    raw_low = d_raw.astype(bf16)
    rawg_ref[...] = raw_low
    d_scores_low = jnp.where(allowed, d_scores, 0.0).astype(bf16)
    d_c = mm(entered_low, state_low, ((1,), (1,))) + mm(d_scores_low, b_low)
    d_b = mm(left_low, d_state_low, ((1,), (1,))) + mm(d_scores_low, c_low, ((0,), (0,)))
    buf[:BLOCK, :INNER] = (dy * skip_ref[...] + d_weighted * step_wide) * slope[:, :INNER]
    buf[:BLOCK, INNER : INNER + STATE] = d_b * slope[:, INNER : INNER + STATE]
    buf[:BLOCK, INNER + STATE :] = d_c * slope[:, INNER + STATE :]
    conv_in = ci_ref[...].astype(f32)
    d_conv = buf[:BLOCK, :]
    dconv_b_ref[...] += total(d_conv)
    dconv_w_ref[3:4, :] += total(conv_in * d_conv)
    d_in = conv_w_ref[3:4, :] * d_conv
    for k in range(1, CONV):
        later = buf[k : BLOCK + k, :] * aux[:, 5 + k : 6 + k]
        d_in = d_in + conv_w_ref[3 - k : 4 - k, :] * later
        dconv_w_ref[3 - k : 4 - k, :] += total(conv_in * later)
    buf[BLOCK:, :] = d_conv[:8, :]
    zx_ref[:, INNER:] = d_in.astype(bf16)
    zx_low = zx_ref[...]
    normed_grad = jnp.concatenate([mm(zx_low, in_ref[0]), mm(zx_low, in_ref[1])], axis=1) + mm(
        raw_low, step_ref[...]
    )
    u = u_ref[...].astype(f32)
    inv = lax.rsqrt(jnp.mean(u * u, axis=-1, keepdims=True) + eps)
    dgain_ref[...] += total(normed_grad * u * inv)
    lifted = normed_grad * gain_ref[...]
    mean_u = jnp.mean(lifted * u, axis=-1, keepdims=True)
    ingrad_ref[...] = (
        g.astype(f32) + inv * lifted - u * (inv * inv * inv * mean_u)
    ).astype(bf16)


def layer(layer_in, segment, cotangent, gain, w_in, conv_w, conv_b, dt_bias, a_log, skip, gate_gain, w_out, w_step):
    tokens, width = layer_in.shape
    blocks = tokens // BLOCK
    proj = WIDE + HEADS
    shifted = [jnp.pad(segment, (k, 0), constant_values=-1)[:tokens] for k in range(CONV)]
    after = [jnp.pad(segment, (0, k), constant_values=-1)[k:] for k in range(CONV)]
    by_block = segment.reshape(blocks, BLOCK)
    before = jnp.concatenate([jnp.full((1,), -1, segment.dtype), by_block[:-1, -1]])
    aux = jnp.stack(
        [shifted[k] == segment for k in (1, 2, 3)]
        + [
            (by_block == before[:, None]).reshape(tokens),
            (by_block == by_block[:, -1:]).reshape(tokens),
            segment,
        ]
        + [after[k] == segment for k in (1, 2, 3)]
        + [segment] * 7,
        axis=1,
    ).astype(f32)
    seg_rows = segment.astype(f32).reshape(blocks, 1, BLOCK)
    pad_head = lambda v: jnp.pad(v.astype(f32), (0, LANES - HEADS))
    heads = jnp.stack([pad_head(dt_bias), pad_head(a_log)] + [jnp.zeros((LANES,), f32)] * 6)
    skip_wide = jnp.repeat(skip.astype(f32), HEADDIM).reshape(1, INNER)
    owner = jnp.arange(INNER) // HEADDIM
    one = (jnp.arange(LANES)[:, None] == owner[None, :]).astype(bf16)
    spread_mat = jnp.concatenate([one, one], axis=0)
    gain_row = gain.astype(f32).reshape(1, width)
    conv_w = conv_w.astype(f32)
    conv_b = conv_b.astype(f32).reshape(1, XBC)
    gate_row = gate_gain.astype(f32).reshape(1, INNER)

    def full(a):
        return pl.BlockSpec(a.shape, lambda i: (0,) * a.ndim, pipeline_mode=pl.Buffered(1))

    def rows(cols, order):
        return pl.BlockSpec((BLOCK, cols), lambda i: (order(i), 0))

    fwd = lambda i: i
    bwd = lambda i: blocks - 1 - i
    shape = jax.ShapeDtypeStruct
    params = pltpu.CompilerParams(
        dimension_semantics=("arbitrary",), vmem_limit_bytes=60 * 1024 * 1024
    )
    normed, gate, conv_in, conv, raw, y, states, mixed, layer_out = pl.pallas_call(
        forward_kernel,
        grid=(blocks,),
        in_specs=[
            rows(width, fwd), rows(16, fwd), pl.BlockSpec((1, 1, BLOCK), lambda i: (i, 0, 0)),
            full(gain_row), full(w_in), full(w_step), full(conv_w), full(conv_b), full(heads),
            full(skip_wide), full(gate_row), full(w_out), full(spread_mat),
        ],
        out_specs=[
            rows(width, fwd), rows(INNER, fwd), rows(XBC, fwd), rows(XBC, fwd), rows(LANES, fwd),
            rows(INNER, fwd), pl.BlockSpec((1, STATE, INNER), lambda i: (i, 0, 0)),
            rows(INNER, fwd), rows(width, fwd),
        ],
        out_shape=[
            shape((tokens, width), bf16), shape((tokens, INNER), f32), shape((tokens, XBC), bf16),
            shape((tokens, XBC), f32), shape((tokens, LANES), f32), shape((tokens, INNER), f32),
            shape((blocks, STATE, INNER), bf16), shape((tokens, INNER), bf16),
            shape((tokens, width), bf16),
        ],
        scratch_shapes=[
            pltpu.VMEM((BLOCK + 8, XBC), f32), pltpu.VMEM((STATE, INNER), f32),
            pltpu.VMEM((BLOCK, INNER), f32),
        ],
        compiler_params=params,
        cost_estimate=pl.CostEstimate(
            flops=2 * tokens * width * (proj + INNER) * 2, bytes_accessed=40_000_000,
            transcendentals=tokens * 8000,
        ),
        name="layer_forward",
    )(layer_in, aux, seg_rows, gain_row, w_in, w_step, conv_w, conv_b, heads, skip_wide, gate_row,
      w_out, spread_mat)
    acc = lambda r, c: pl.BlockSpec((r, c), lambda i: (0, 0))
    input_grad, zx_grad, raw_grad, d_gain, d_conv_w, d_conv_b, d_heads, d_skip, d_gate_gain = (
        pl.pallas_call(
            backward_kernel,
            grid=(blocks,),
            in_specs=[
                rows(width, bwd), rows(width, bwd), rows(16, bwd),
                pl.BlockSpec((1, 1, BLOCK), lambda i: (blocks - 1 - i, 0, 0)),
                full(gain_row), full(w_in), full(w_step), full(conv_w), full(heads),
                full(skip_wide), full(gate_row), full(w_out), full(spread_mat),
                rows(INNER, bwd), rows(XBC, bwd), rows(XBC, bwd), rows(LANES, bwd),
                rows(INNER, bwd),
                pl.BlockSpec((1, STATE, INNER), lambda i: (blocks - 1 - i, 0, 0)),
            ],
            out_specs=[
                rows(width, bwd), rows(WIDE, bwd), rows(LANES, bwd), acc(1, width), acc(CONV, XBC),
                acc(1, XBC), acc(8, LANES), acc(1, INNER), acc(1, INNER),
            ],
            out_shape=[
                shape((tokens, width), bf16), shape((tokens, WIDE), bf16),
                shape((tokens, LANES), bf16), shape((1, width), f32), shape((CONV, XBC), f32),
                shape((1, XBC), f32), shape((8, LANES), f32), shape((1, INNER), f32),
                shape((1, INNER), f32),
            ],
            scratch_shapes=[
                pltpu.VMEM((BLOCK + 8, XBC), f32), pltpu.VMEM((STATE, INNER), f32),
                pltpu.VMEM((BLOCK, INNER), f32),
            ],
            compiler_params=params,
            cost_estimate=pl.CostEstimate(
                flops=2 * tokens * width * (proj + INNER) * 3, bytes_accessed=40_000_000,
                transcendentals=tokens * 8000,
            ),
            name="layer_backward",
        )(layer_in, cotangent, aux, seg_rows, gain_row, w_in, w_step, conv_w, heads, skip_wide,
          gate_row, w_out, spread_mat, gate, conv_in, conv, raw, y, states)
    )
    small = (
        d_gain.reshape(width), d_conv_w, d_conv_b.reshape(XBC), d_heads[0, :HEADS],
        d_heads[1, :HEADS], d_skip.reshape(HEADS, HEADDIM).sum(axis=1), d_gate_gain.reshape(INNER),
    )
    return layer_out, input_grad, normed, mixed, zx_grad, raw_grad, small


def exchange_ids():
    s, r = lax.axis_index("shard"), lax.axis_index("rep")
    flip = lambda b: r + b - 2 * b * (lax.rem(lax.div(r, b), 2))
    return s, r, flip


def meet(peers):
    barrier = pltpu.get_barrier_semaphore()
    for peer in peers:
        pl.semaphore_signal(barrier, inc=1, device_id=peer, device_id_type=MESH)
    pl.semaphore_wait(barrier, len(peers))


def gather_kernel(
    pieces, w_ref, o_ref, p_ref, w_all, o_all, p_all, w_stage, o_stage, p_stage, local_sem,
    p_sem, send_sem, recv_sem,
):
    s, r, flip = exchange_ids()
    y_peer, x_peer, c_peer = (1 - s, r), (s, flip(2)), (s, flip(1))
    meet((y_peer, x_peer, c_peer))
    quarter = lax.rem(r, 4)
    x_quarter = lax.rem(flip(2), 4)

    def place(which, shard, part, piece):
        rows = pieces[which]
        at = pl.multiple_of((part * len(rows[1]) + piece) * rows[0], 16)
        if which == 0:
            return w_all.at[shard, pl.ds(at, rows[0])]
        return o_all.at[shard, pl.ds(at, rows[0])]

    def source(which, part, piece):
        rows = pieces[which]
        at = pl.multiple_of((part * len(rows[1]) + piece) * rows[0], 16)
        return (w_ref, o_ref)[which].at[pl.ds(at, rows[0])]

    todo = [(which, piece) for which in range(2) for piece in pieces[which][1]]
    small = pltpu.make_async_remote_copy(
        p_ref, p_all.at[s], p_sem.at[0], p_sem.at[1], device_id=y_peer, device_id_type=MESH
    )
    small.start()
    first = []
    for k, (which, piece) in enumerate(todo):
        copy = pltpu.make_async_remote_copy(
            source(which, quarter, piece), place(which, s, quarter, piece),
            send_sem.at[0, k], recv_sem.at[0, k], device_id=y_peer, device_id_type=MESH,
        )
        copy.start()
        first.append(copy)
    own = []
    stages = ((p_ref, p_stage, p_all), (w_ref, w_stage, w_all), (o_ref, o_stage, o_all))
    into = [pltpu.make_async_copy(a, b, local_sem.at[0, i]) for i, (a, b, _) in enumerate(stages)]
    for copy in into:
        copy.start()
    for i, (_, b, c) in enumerate(stages):
        into[i].wait()
        own.append(pltpu.make_async_copy(b, c.at[s], local_sem.at[1, i]))
        own[i].start()
    away = 1 - s
    second, third = [], []

    def pass_on(k, which, piece, part, lane, peer):
        block = place(which, away, part, piece)
        copy = pltpu.make_async_remote_copy(
            block, block, send_sem.at[lane, k], recv_sem.at[lane, k], device_id=peer,
            device_id_type=MESH,
        )
        copy.start()
        return copy

    def take_x(k):
        which, piece = todo[k]
        second[k].wait_recv()
        third.append(pass_on(k, which, piece, x_quarter, 3, c_peer))

    near = []
    for k, (which, piece) in enumerate(todo):
        first[k].wait_recv()
        second.append(pass_on(k, which, piece, quarter, 1, x_peer))
        near.append(pass_on(k, which, piece, quarter, 2, c_peer))
        if k > 0:
            take_x(k - 1)
    take_x(len(todo) - 1)
    for copy in near + third:
        copy.wait()
    for copy in first + second:
        copy.wait_send()
    for copy in own:
        copy.wait()
    small.wait()


def gather(w_t, w_out, pack):
    pieces = []
    for a, count in ((w_t, 4), (w_out, 2)):
        pieces.append((a.shape[0] // (4 * count), tuple(range(count))))
    n = sum(len(p[1]) for p in pieces)
    any_spec = pl.BlockSpec(memory_space=pl.ANY)
    return pl.pallas_call(
        functools.partial(gather_kernel, pieces),
        out_shape=[jax.ShapeDtypeStruct((2,) + a.shape, a.dtype) for a in (w_t, w_out, pack)],
        in_specs=[any_spec] * 3,
        out_specs=[any_spec] * 3,
        scratch_shapes=[pltpu.VMEM(a.shape, a.dtype) for a in (w_t, w_out, pack)]
        + [
            pltpu.SemaphoreType.DMA((2, 3)), pltpu.SemaphoreType.DMA((2,)),
            pltpu.SemaphoreType.DMA((4, n)), pltpu.SemaphoreType.DMA((4, n)),
        ],
        compiler_params=pltpu.CompilerParams(
            collective_id=0, has_side_effects=True, vmem_limit_bytes=16 * 1024 * 1024
        ),
        name="gather_weights",
    )(w_t, w_out, pack)


def reduce_kernel(plan, m, count, *refs):
    ins = refs[:count]
    outs = refs[count : 2 * count]
    rest = refs[2 * count :]
    from_c, from_y, from_x, from_z = (rest[i * count : (i + 1) * count] for i in range(4))
    send_sem, recv_sem, zs_sem, zr_sem = rest[4 * count :]
    s, r, flip = exchange_ids()
    core, xbit = lax.rem(r, 2), lax.rem(lax.div(r, 2), 2)
    zed = lax.div(r, 4)
    y_peer, x_peer, c_peer = (1 - s, r), (s, flip(2)), (s, flip(1))

    def z_peer(d):
        return (s, lax.rem(zed + d, m) * 4 + lax.rem(r, 4))

    meet((y_peer, x_peer, c_peer) + tuple(z_peer(d) for d in range(1, m)))

    def remote(src, dst, lane, k, peer):
        copy = pltpu.make_async_remote_copy(
            src, dst, send_sem.at[lane, k], recv_sem.at[lane, k], device_id=peer, device_id_type=MESH
        )
        copy.start()
        return copy

    def span(at, size):
        return pl.ds(pl.multiple_of(at, 8 if size % 16 else 16), size)

    live = [dict() for _ in plan]

    def stage(k, step):
        which, start, size = plan[k]
        x, out = ins[which], outs[which]
        rc, ry, rx, rz = (b[which] for b in (from_c, from_y, from_x, from_z))
        half, fourth, part = size // 2, size // 4, size // (4 * m)
        c_at, y_at, x_at, z_at = start, start // 2, start // 4, start // (4 * m)
        mine = start + core * half
        mine_x = mine + xbit * fourth
        mine_z = mine_x + zed * part
        held = live[k]
        f = lambda v: v.astype(f32)
        if step == 0:
            held[0] = remote(
                x.at[:, span(start + (1 - core) * half, half)], rc.at[:, span(y_at, half)], 0, k, c_peer
            )
        elif step == 1:
            held[0].wait_recv()
            both_rows = pl.ds(y_at, half)
            rc[:, both_rows] = (
                f(rc[:, both_rows]) + f(x[:, span(mine, half)])
            ).astype(x.dtype)
            held[1] = remote(rc.at[1 - s, both_rows], ry.at[both_rows], 1, k, y_peer)
        elif step == 2:
            held[1].wait_recv()
            rows = pl.ds(y_at, half)
            ry[rows] = (f(ry[rows]) + f(rc[s, rows])).astype(x.dtype)
            held[2] = remote(
                ry.at[span(y_at + (1 - xbit) * fourth, fourth)], rx.at[pl.ds(x_at, fourth)], 2, k, x_peer
            )
        elif step == 3:
            held[2].wait_recv()
            rows = pl.ds(x_at, fourth)
            rx[rows] = (f(rx[rows]) + f(ry[span(y_at + xbit * fourth, fourth)])).astype(x.dtype)
            held[3] = []
            for d in range(1, m):
                there = lax.rem(zed + d, m)
                copy = pltpu.make_async_remote_copy(
                    rx.at[span(x_at + there * part, part)], rz.at[d - 1, pl.ds(z_at, part)],
                    zs_sem.at[0, k, d - 1], zr_sem.at[0, k, d - 1], device_id=z_peer(d),
                    device_id_type=MESH,
                )
                copy.start()
                held[3].append(copy)
        elif step == 4:
            total = f(rx[span(x_at + zed * part, part)])
            for d in range(1, m):
                held[3][d - 1].wait_recv()
                total = total + f(rz[d - 1, pl.ds(z_at, part)])
            rows = span(mine_z, part)
            out[rows] = total.astype(x.dtype)
            held[4] = []
            for d in range(1, m):
                copy = pltpu.make_async_remote_copy(
                    out.at[rows], out.at[rows],
                    zs_sem.at[1, k, d - 1], zr_sem.at[1, k, d - 1], device_id=z_peer(d),
                    device_id_type=MESH,
                )
                copy.start()
                held[4].append(copy)
        elif step == 5:
            for copy in held[4]:
                copy.wait_recv()
            block = out.at[span(mine_x, fourth)]
            held[5] = remote(block, block, 3, k, x_peer)
        elif step == 6:
            held[5].wait_recv()
            block = out.at[span(mine, half)]
            held[6] = remote(block, block, 4, k, c_peer)
        else:
            held[6].wait_recv()
            for i in (0, 1, 2, 5, 6):
                held[i].wait_send()
            for copy in held[3] + held[4]:
                copy.wait_send()

    for tick in range(len(plan) + 7):
        for k in range(len(plan)):
            if 0 <= tick - k < 8:
                stage(k, tick - k)


def reduce_all(arrays, counts, ident, name):
    m = lax.axis_size("rep") // 4
    padded, plan = [], []
    for which, (a, c) in enumerate(zip(arrays, counts)):
        unit = (16 if a.dtype == bf16 else 8) * 4 * m
        units = -(-a.shape[1] // unit)
        padded.append(jnp.pad(a, ((0, 0), (0, units * unit - a.shape[1]), (0, 0))))
        at = 0
        for i in range(min(c, units)):
            size = units * (i + 1) // min(c, units) * unit - at
            plan.append((which, at, size))
            at += size
    vmem = pl.BlockSpec(memory_space=pltpu.VMEM)
    n = len(arrays)
    scratch = []
    for shape in (
        lambda a: (2, a.shape[1] // 2, a.shape[2]), lambda a: (a.shape[1] // 2, a.shape[2]),
        lambda a: (a.shape[1] // 4, a.shape[2]),
        lambda a: (max(m - 1, 1), a.shape[1] // (4 * m), a.shape[2]),
    ):
        scratch += [pltpu.VMEM(shape(a), a.dtype) for a in padded]
    outs = pl.pallas_call(
        functools.partial(reduce_kernel, tuple(plan), m, n),
        out_shape=[jax.ShapeDtypeStruct(a.shape[1:], a.dtype) for a in padded],
        in_specs=[vmem] * n,
        out_specs=[vmem] * n,
        scratch_shapes=scratch
        + [
            pltpu.SemaphoreType.DMA((5, len(plan))), pltpu.SemaphoreType.DMA((5, len(plan))),
            pltpu.SemaphoreType.DMA((2, len(plan), max(m - 1, 1))),
            pltpu.SemaphoreType.DMA((2, len(plan), max(m - 1, 1))),
        ],
        compiler_params=pltpu.CompilerParams(
            collective_id=ident, has_side_effects=True, vmem_limit_bytes=56 * 1024 * 1024
        ),
        name=name,
    )(*padded)
    return [o[: a.shape[1]] for o, a in zip(outs, arrays)]


def body(
    layer_in, segment_ids, cotangent, norm_gain, in_weight, conv_weight, conv_bias, dt_bias, a_log,
    skip_gain, gate_gain, out_weight,
):
    vectors = (norm_gain, conv_weight, conv_bias, dt_bias, a_log, skip_gain, gate_gain)
    w_t = in_weight.T
    step_t = w_t[WIDE:]
    flat = jnp.concatenate([step_t.reshape(-1)] + [v.reshape(-1) for v in vectors])
    rows = -(-flat.size // (16 * LANES)) * 16
    pack = jnp.pad(flat, (0, rows * LANES - flat.size)).reshape(rows, LANES)
    w_all, o_all, p_all = gather(w_t[:WIDE], out_weight, pack)
    packed = p_all.reshape(2, -1)
    w_step = packed[:, : step_t.size].reshape((2,) + step_t.shape).transpose(1, 0, 2)
    w_step = jnp.pad(w_step.reshape(HEADS, -1), ((0, LANES - HEADS), (0, 0)))
    whole, at = [], step_t.size
    for v in vectors:
        piece = packed[:, at : at + v.size]
        at += v.size
        if v.ndim == 2:
            piece = piece.reshape((-1,) + v.shape).transpose(1, 0, 2).reshape(v.shape[0], -1)
        else:
            piece = piece.reshape(-1)
        whole.append(piece)
    gain, conv_w, conv_b, step_bias, alog, skip, gate_vec = whole
    layer_out, input_grad, normed, mixed, zx_grad, raw_grad, small = layer(
        layer_in, segment_ids.reshape(-1), cotangent, gain, w_all, conv_w, conv_b, step_bias, alog,
        skip, gate_vec, o_all.reshape(INNER, -1), w_step,
    )
    factor = 1.0 / (lax.axis_size("shard") * lax.axis_size("rep"))
    width = layer_in.shape[1]
    nt = ((0,), (0,))
    out_grad = mm(mixed, cotangent, nt).astype(bf16).reshape(2, -1, width)
    half = width // 2
    in_grad = jnp.stack([mm(zx_grad, normed[:, i * half : (i + 1) * half], nt) for i in range(2)]).astype(bf16)
    step_grad = mm(raw_grad[:, :HEADS], normed, nt)
    per_shard = [step_grad.reshape(HEADS, 2, half).transpose(1, 0, 2).reshape(2, -1)]
    for v in small:
        if v.ndim == 2:
            per_shard.append(v.reshape(v.shape[0], 2, -1).transpose(1, 0, 2).reshape(2, -1))
        else:
            per_shard.append(v.reshape(2, -1))
    flat = jnp.concatenate(per_shard, axis=1)
    rows = -(-flat.shape[1] // LANES)
    flat = jnp.pad(flat, ((0, 0), (0, rows * LANES - flat.shape[1]))).reshape(2, rows, LANES)
    small_sum, in_sum, out_sum = reduce_all([flat, in_grad, out_grad], (1, 4, 2), 1, "reduce_grads")
    small_sum = small_sum.reshape(-1) * factor
    step_sum = small_sum[: step_t.size].reshape(step_t.shape)
    in_weight_grad = jnp.concatenate([in_sum.astype(f32) * factor, step_sum], axis=0).T
    outs, at = [], step_t.size
    for v in vectors:
        outs.append(small_sum[at : at + v.size].reshape(v.shape))
        at += v.size
    return (
        layer_out, input_grad, outs[0], in_weight_grad, outs[1], outs[2], outs[3],
        outs[4], outs[5], outs[6], out_sum.astype(f32) * factor,
    )


def solution(mesh):
    in_specs = (
        P(("shard", "rep"), None),
        P(("shard", "rep"), None),
        P(("shard", "rep"), None),
        P("shard"),
        P("shard", None),
        P(None, "shard"),
        P("shard"),
        P("shard"),
        P("shard"),
        P("shard"),
        P("shard"),
        P("shard", None),
    )
    out_specs = (
        P(("shard", "rep"), None),
        P(("shard", "rep"), None),
        P("shard"),
        P("shard", None),
        P(None, "shard"),
        P("shard"),
        P("shard"),
        P("shard"),
        P("shard"),
        P("shard"),
        P("shard", None),
    )
    return jax.shard_map(body, mesh=mesh, in_specs=in_specs, out_specs=out_specs, check_vma=False)
```

```python
import functools

import jax
import jax.numpy as jnp
from jax import lax
from jax.experimental import pallas as pl
from jax.experimental.pallas import tpu as pltpu
from jax.sharding import PartitionSpec as P

HEADS = 24
HEADDIM = 64
STATE = 128
CONV = 4
BLOCK = 128
INNER = 1536
XBC = 1792
WIDE = INNER + XBC
LANES = 128
LOG2E = 1.4426950408889634

MESH = pl.DeviceIdType.MESH
eps = 1e-05
highest = lax.Precision.HIGHEST
f32 = jnp.float32
bf16 = jnp.bfloat16


def mm(a, b, contract=((1,), (0,))):
    return lax.dot_general(a, b, (contract, ((), ())), preferred_element_type=f32)


def mm_t(a, w_ref):
    half = w_ref.shape[2]
    nt = ((1,), (1,))
    return mm(a[:, :half], w_ref[0], nt) + mm(a[:, half:], w_ref[1], nt)


def total(v):
    return jnp.sum(v, axis=0, keepdims=True)


def sigmoid(v):
    return 0.5 + 0.5 * jnp.tanh(0.5 * v)


def softplus(v):
    small = jnp.exp(-jnp.abs(v))
    series = small * (1.0 - small * (0.5 - small * (1.0 / 3.0 - small * 0.25)))
    return jnp.maximum(v, 0.0) + jnp.where(small < 0.03, series, jnp.log(1.0 + small))


def spread(per_head, spread_mat):
    high = per_head.astype(bf16)
    rest = (per_head - high.astype(f32)).astype(bf16)
    return mm(jnp.concatenate([high, rest], axis=1), spread_mat)


def gain_row(p):
    return jnp.concatenate([p[i, j : j + 1, :] for i in range(2) for j in range(3)], axis=1)


def conv_tap(p, tap, j):
    at = 3 + tap * 7 + j % 7
    return p[j // 7, at : at + 1, :]


def conv_bias(p, j):
    return p[j // 7, 31 + j % 7 : 32 + j % 7, :]


def skip_row(p, pair):
    return p[pair // 6, 38 + pair % 6 : 39 + pair % 6, :]


def gate_row(p, pair):
    return p[pair // 6, 44 + pair % 6 : 45 + pair % 6, :]


def head_row(p, k):
    return p[0, 50 + k : 51 + k, :] + p[1, 50 + k : 51 + k, :]


def lane_pair(values, first):
    lane = lax.broadcasted_iota(jnp.int32, values.shape, 1)
    zero = jnp.zeros_like(values)
    return jnp.concatenate(
        [jnp.where(lane < HEADDIM, values, zero), jnp.where(lane >= HEADDIM, values, zero)], axis=0
    )


def spread_of(running, running_t, head):
    diff = running[:, head : head + 1] - running_t[head : head + 1, :]
    return jnp.exp2(jnp.minimum(diff, 0.0))


def spread_back(running, running_t, head):
    diff = running_t[head : head + 1, :] - running[:, head : head + 1]
    return jnp.exp2(jnp.minimum(diff, 0.0))


def exchange_ids():
    s, r = lax.axis_index("shard"), lax.axis_index("rep")
    flip = lambda b: r + b - 2 * b * (lax.rem(lax.div(r, b), 2))
    return s, r, flip


def meet(peers):
    barrier = pltpu.get_barrier_semaphore()
    for peer in peers:
        pl.semaphore_signal(barrier, inc=1, device_id=peer, device_id_type=MESH)
    pl.semaphore_wait(barrier, len(peers))


def gather_kernel(
    pieces, w_ref, o_ref, d_ref, p_ref, c_all, g_all, o_all, d_all, p_all, w_stage, o_stage, d_stage, p_stage,
    local_sem, small_sem, send_sem, recv_sem,
):
    s, r, flip = exchange_ids()
    y_peer, x_peer, c_peer = (1 - s, r), (s, flip(2)), (s, flip(1))
    meet((y_peer, x_peer, c_peer))
    quarter = lax.rem(r, 4)
    x_quarter = lax.rem(flip(2), 4)
    sections = ((w_ref, INNER, c_all), (w_ref, 0, g_all), (o_ref, 0, o_all))
    todo = [(which, piece) for which, (_, count) in enumerate(pieces) for piece in range(count)]

    def rows_at(which, part, piece, base=0):
        size, count = pieces[which]
        return pl.ds(pl.multiple_of(base + (part * count + piece) * size, 16), size)

    def place(which, shard, part, piece):
        return sections[which][2].at[shard, rows_at(which, part, piece)]

    small = []
    for i, (src, dst) in enumerate(((d_ref, d_all), (p_ref, p_all))):
        copy = pltpu.make_async_remote_copy(
            src, dst.at[s], small_sem.at[0, i], small_sem.at[1, i], device_id=y_peer, device_id_type=MESH
        )
        copy.start()
        small.append(copy)
    first = []
    for k, (which, piece) in enumerate(todo):
        src, base, _ = sections[which]
        copy = pltpu.make_async_remote_copy(
            src.at[rows_at(which, quarter, piece, base)], place(which, s, quarter, piece),
            send_sem.at[0, k], recv_sem.at[0, k], device_id=y_peer, device_id_type=MESH,
        )
        copy.start()
        first.append(copy)
    stages = (
        (d_ref, d_stage, d_all.at[s]), (p_ref, p_stage, p_all.at[s]),
        (w_ref.at[pl.ds(INNER, XBC)], w_stage.at[pl.ds(INNER, XBC)], c_all.at[s]),
        (w_ref.at[pl.ds(0, INNER)], w_stage.at[pl.ds(0, INNER)], g_all.at[s]),
        (o_ref, o_stage, o_all.at[s]),
    )
    into = [pltpu.make_async_copy(a, b, local_sem.at[0, i]) for i, (a, b, _) in enumerate(stages)]
    for copy in into:
        copy.start()
    own = []
    for i, (_, b, c) in enumerate(stages):
        into[i].wait()
        own.append(pltpu.make_async_copy(b, c, local_sem.at[1, i]))
        own[i].start()
    away = 1 - s
    second, third = [], []

    def pass_on(k, which, piece, part, lane, peer):
        block = place(which, away, part, piece)
        copy = pltpu.make_async_remote_copy(
            block, block, send_sem.at[lane, k], recv_sem.at[lane, k], device_id=peer,
            device_id_type=MESH,
        )
        copy.start()
        return copy

    def take_x(k):
        which, piece = todo[k]
        second[k].wait_recv()
        third.append(pass_on(k, which, piece, x_quarter, 3, c_peer))

    near = []
    for k, (which, piece) in enumerate(todo):
        first[k].wait_recv()
        second.append(pass_on(k, which, piece, quarter, 1, x_peer))
        near.append(pass_on(k, which, piece, quarter, 2, c_peer))
        if k > 0:
            take_x(k - 1)
    take_x(len(todo) - 1)
    for copy in near + third:
        copy.wait()
    for copy in first + second:
        copy.wait_send()
    for copy in own + small:
        copy.wait()


def gather(w_t, w_out, step_t, pack):
    half, width = w_t.shape[1], w_out.shape[1]
    any_spec = pl.BlockSpec(memory_space=pl.ANY)
    pieces = ((XBC // 16, 4), (INNER // 12, 3), (w_out.shape[0] // 12, 3))
    n = sum(count for _, count in pieces)
    out = [(XBC, half), (INNER, half), w_out.shape, step_t.shape, pack.shape]
    return pl.pallas_call(
        functools.partial(gather_kernel, pieces),
        out_shape=[jax.ShapeDtypeStruct((2,) + tuple(o), bf16) for o in out],
        in_specs=[any_spec] * 4,
        out_specs=[any_spec] * 5,
        scratch_shapes=[
            pltpu.VMEM((WIDE, half), bf16), pltpu.VMEM(w_out.shape, bf16), pltpu.VMEM(step_t.shape, bf16),
            pltpu.VMEM(pack.shape, bf16),
            pltpu.SemaphoreType.DMA((2, 5)), pltpu.SemaphoreType.DMA((2, 2)),
            pltpu.SemaphoreType.DMA((4, n)), pltpu.SemaphoreType.DMA((4, n)),
        ],
        compiler_params=pltpu.CompilerParams(
            collective_id=0, has_side_effects=True, vmem_limit_bytes=16 * 1024 * 1024
        ),
        name="gather_weights",
    )(w_t, w_out, step_t, pack)


def k1_kernel(
    u_ref, aux_ref, c_ref, d_ref, p_ref, spread_ref,
    normed_ref, ci_ref, conv_ref, raw_ref, run_ref, y_ref, state_ref,
    buf, hidden, wide, inter,
):
    @pl.when(pl.program_id(0) == 0)
    def _():
        buf[0:8, :] = jnp.zeros((8, XBC), f32)
        hidden[...] = jnp.zeros_like(hidden)

    p = p_ref[...].astype(f32)
    u = u_ref[...].astype(f32)
    inv = lax.rsqrt(jnp.mean(u * u, axis=-1, keepdims=True) + eps)
    normed = (u * inv * gain_row(p)).astype(bf16)
    normed_ref[...] = normed
    buf[8 : 8 + BLOCK, :] = mm_t(normed, c_ref)
    raw = mm_t(normed, d_ref)
    raw_ref[:, : raw.shape[1]] = raw
    raw_ref[:, raw.shape[1] :] = jnp.zeros((BLOCK, LANES - raw.shape[1]), f32)
    aux = jnp.transpose(aux_ref[0])
    masks = [jnp.broadcast_to(aux[:, k : k + 1], (BLOCK, LANES)) for k in range(3)]
    step = softplus(raw_ref[...] + head_row(p, 0))
    decay = (-LOG2E) * jnp.exp(head_row(p, 1)) * step
    row = lax.broadcasted_iota(jnp.int32, (BLOCK, BLOCK), 0)
    col = lax.broadcasted_iota(jnp.int32, (BLOCK, BLOCK), 1)
    lower = (row >= col).astype(f32)
    running = lax.dot_general(
        lower, decay, (((1,), (0,)), ((), ())), precision=highest, preferred_element_type=f32
    )
    run_ref[...] = running
    running_t = jnp.transpose(running)
    entering = jnp.exp2(running) * aux[:, 3:4]
    leaving = jnp.exp2(running[BLOCK - 1 : BLOCK, :] - running) * aux[:, 4:5]
    wide[...] = spread(jnp.concatenate([step, entering, leaving], axis=0), spread_ref[...])

    def conv_chunk(j):
        cols = slice(j * LANES, (j + 1) * LANES)
        x = buf[8 : 8 + BLOCK, cols]
        ci_ref[:, cols] = x.astype(bf16)
        conv = conv_bias(p, j) + conv_tap(p, CONV - 1, j) * x
        for k in range(1, CONV):
            conv = conv + conv_tap(p, CONV - 1 - k, j) * (buf[8 - k : 8 - k + BLOCK, cols] * masks[k - 1])
        conv_ref[:, cols] = conv
        return conv * sigmoid(conv)

    b_low = conv_chunk(HEADS // 2).astype(bf16)
    c_low = conv_chunk(HEADS // 2 + 1).astype(bf16)
    b_t = jnp.transpose(b_low)
    allowed = (row >= col) & (aux[:, 5:6] == aux_ref[0, 5:6, :])
    scores = jnp.where(allowed, mm(c_low, b_low, ((1,), (1,))), 0.0)
    state_low = hidden[...].astype(bf16)
    state_ref[0] = state_low
    inter[...] = mm(c_low, state_low)
    for pair in range(HEADS // 2):
        cols = slice(pair * LANES, (pair + 1) * LANES)
        values = conv_chunk(pair)
        weighted = values * wide[0:BLOCK, cols]
        first = (spread_of(running, running_t, 2 * pair) * scores).astype(bf16)
        second = (spread_of(running, running_t, 2 * pair + 1) * scores).astype(bf16)
        enter = wide[BLOCK : 2 * BLOCK, cols]
        y_ref[:, cols] = (
            mm(jnp.concatenate([first, second], axis=1), lane_pair(weighted.astype(bf16), pair))
            + inter[:, cols] * enter
            + skip_row(p, pair) * values
        )
        left = (weighted * wide[2 * BLOCK :, cols]).astype(bf16)
        hidden[:, cols] = hidden[:, cols] * wide[2 * BLOCK - 1 : 2 * BLOCK, cols] + mm(b_t, left)
    buf[0:8, :] = buf[BLOCK : BLOCK + 8, :]


def k2_kernel(
    u_ref, normed_ref, g_ref, y_ref, g_all_ref, o_ref, p_ref,
    out_ref, mixed_ref, dy_ref, zx_ref, dgate_ref,
    gate, mixed_grad, gated, sig,
):
    rows = u_ref.shape[0]

    @pl.when(pl.program_id(0) == 0)
    def _():
        dgate_ref[...] = jnp.zeros_like(dgate_ref)

    p = p_ref[...].astype(f32)
    gate[...] = mm_t(normed_ref[...], g_all_ref)
    out_w = o_ref[...].reshape(INNER, -1)
    mixed_grad[...] = mm(g_ref[...], out_w, ((1,), (1,)))
    SUB = 64
    for sub in range(rows // SUB):
        r = slice(sub * SUB, (sub + 1) * SUB)
        square = jnp.zeros((SUB, LANES), f32)
        cross = jnp.zeros((SUB, LANES), f32)
        for pair in range(HEADS // 2):
            cols = slice(pair * LANES, (pair + 1) * LANES)
            v = gate[r, cols]
            s = sigmoid(v)
            sig[r, cols] = s
            product = y_ref[r, cols] * (v * s)
            gated[r, cols] = product
            square = square + product * product
            cross = cross + mixed_grad[r, cols] * gate_row(p, pair) * product
        inv = lax.rsqrt(jnp.sum(square, axis=-1, keepdims=True) * (1.0 / INNER) + eps)
        back = inv * inv * inv * (jnp.sum(cross, axis=-1, keepdims=True) * (1.0 / INNER))
        inv = jnp.broadcast_to(inv, (SUB, LANES))
        back = jnp.broadcast_to(back, (SUB, LANES))
        for pair in range(HEADS // 2):
            cols = slice(pair * LANES, (pair + 1) * LANES)
            v, s, product = gate[r, cols], sig[r, cols], gated[r, cols]
            scaled = product * inv
            gain = gate_row(p, pair)
            mixed_ref[r, cols] = (scaled * gain).astype(bf16)
            mg = mixed_grad[r, cols]
            dgate_ref[pair // 6, pair % 6 : pair % 6 + 1, :] += total(mg * scaled)
            d_gated = inv * (mg * gain) - product * back
            act = v * s
            dy_ref[r, cols] = d_gated * act
            zx_ref[r, cols] = (d_gated * y_ref[r, cols] * (s + act * (1.0 - s))).astype(bf16)
    out_ref[...] = (u_ref[...].astype(f32) + mm(mixed_ref[...], out_w)).astype(bf16)


def scan_back_step(
    here, aux_ref, p_ref, spread_ref, ci_ref, conv_ref, raw_ref, run_ref, y_ref, dy_ref, state_ref,
    zx_all, rawg_all, dp_ref, buf, d_hidden, wide, d_left, entered, left, sums,
):
    p = p_ref[...].astype(f32)
    aux = jnp.transpose(aux_ref[0])
    masks = [jnp.broadcast_to(aux[:, k : k + 1], (BLOCK, LANES)) for k in range(6, 9)]
    pre = raw_ref[...] + head_row(p, 0)
    step = softplus(pre)
    rate = -jnp.exp(head_row(p, 1))
    running = run_ref[...]
    running_t = jnp.transpose(running)
    entering = jnp.exp2(running) * aux[:, 3:4]
    leaving = jnp.exp2(running[BLOCK - 1 : BLOCK, :] - running) * aux[:, 4:5]
    spread_mat = spread_ref[...]
    wide[...] = spread(jnp.concatenate([step, entering, leaving], axis=0), spread_mat)

    def act_chunk(j):
        cols = slice(j * LANES, (j + 1) * LANES)
        conv = conv_ref[:, cols]
        sig = sigmoid(conv)
        act = conv * sig
        return act, sig + act * (1.0 - sig)

    def conv_back(j, d_conv):
        cols = slice(j * LANES, (j + 1) * LANES)
        buf[:BLOCK, cols] = d_conv
        ci = ci_ref[:, cols].astype(f32)
        shard, at = j // 7, j % 7
        dp_ref[shard, 31 + at : 32 + at, :] += total(d_conv)
        dp_ref[shard, 24 + at : 25 + at, :] += total(ci * d_conv)
        d_in = conv_tap(p, CONV - 1, j) * d_conv
        for k in range(1, CONV):
            later = buf[k : BLOCK + k, cols] * masks[k - 1]
            d_in = d_in + conv_tap(p, CONV - 1 - k, j) * later
            row_at = 3 + (CONV - 1 - k) * 7 + at
            dp_ref[shard, row_at : row_at + 1, :] += total(ci * later)
        zx_all[here, cols] = d_in.astype(bf16)
        buf[BLOCK:, cols] = d_conv[:8, :]

    b_act, b_slope = act_chunk(HEADS // 2)
    c_act, c_slope = act_chunk(HEADS // 2 + 1)
    b_low, c_low = b_act.astype(bf16), c_act.astype(bf16)
    c_t = jnp.transpose(c_low)
    row = lax.broadcasted_iota(jnp.int32, (BLOCK, BLOCK), 0)
    col = lax.broadcasted_iota(jnp.int32, (BLOCK, BLOCK), 1)
    allowed_t = (col >= row) & (aux[:, 5:6] == aux_ref[0, 5:6, :])
    scores_t = jnp.where(allowed_t, mm(b_low, c_low, ((1,), (1,))), 0.0)
    d_state_low = d_hidden[...].astype(bf16)
    d_left[...] = mm(b_low, d_state_low)
    d_scores_t = jnp.zeros((BLOCK, BLOCK), f32)
    for pair in range(HEADS // 2):
        cols = slice(pair * LANES, (pair + 1) * LANES)
        values, slope = act_chunk(pair)
        step_wide = wide[0:BLOCK, cols]
        enter = wide[BLOCK : 2 * BLOCK, cols]
        leave = wide[2 * BLOCK :, cols]
        dy = dy_ref[:, cols]
        skip = skip_row(p, pair)
        weighted = values * step_wide
        left[:, cols] = (weighted * leave).astype(bf16)
        entered_low = (dy * enter).astype(bf16)
        entered[:, cols] = entered_low
        dp_ref[pair // 6, 38 + pair % 6 : 39 + pair % 6, :] += total(dy * values)
        dy_low = dy.astype(bf16)
        w_low = weighted.astype(bf16)
        d_kernel = mm(lane_pair(w_low, pair), dy_low, ((1,), (1,)))
        spread_a = spread_back(running, running_t, 2 * pair)
        spread_b = spread_back(running, running_t, 2 * pair + 1)
        d_scores_t = d_scores_t + (d_kernel[:BLOCK] * spread_a + d_kernel[BLOCK:] * spread_b)
        kernel_two = jnp.concatenate(
            [(spread_a * scores_t).astype(bf16), (spread_b * scores_t).astype(bf16)], axis=1
        )
        d_leave = d_left[:, cols] * leave
        d_weighted = mm(kernel_two, lane_pair(dy_low, pair)) + d_leave
        w_kept = w_low.astype(f32)
        flow_in = dy_low.astype(f32) * (y_ref[:, cols] - skip * values) - w_kept * d_weighted
        flow_out = d_weighted * values
        for k, flow in enumerate((flow_in, flow_out)):
            high = flow.astype(bf16)
            sums[2 * k * BLOCK : (2 * k + 1) * BLOCK, cols] = high
            sums[(2 * k + 1) * BLOCK : (2 * k + 2) * BLOCK, cols] = (flow - high.astype(f32)).astype(bf16)
        carried = wide[2 * BLOCK - 1 : 2 * BLOCK, cols]
        d_state = d_hidden[:, cols]
        end = total(w_kept * d_leave) + total(d_state * state_ref[0, :, cols].astype(f32)) * carried
        high = end.astype(bf16)
        sums[4 * BLOCK : 4 * BLOCK + 16, cols] = jnp.broadcast_to(high, (16, LANES))
        sums[4 * BLOCK + 16 :, cols] = jnp.broadcast_to((end - high.astype(f32)).astype(bf16), (16, LANES))
        d_hidden[:, cols] = d_state * carried + mm(c_t, entered_low)
        conv_back(pair, (dy * skip + d_weighted * step_wide) * slope)
    d_scores_low = jnp.where(allowed_t, d_scores_t, 0.0).astype(bf16)
    state_low = state_ref[0]
    d_b = mm(left[...], d_state_low, ((1,), (1,))) + mm(d_scores_low, c_low)
    d_c = mm(entered[...], state_low, ((1,), (1,))) + mm(d_scores_low, b_low, ((0,), (0,)))
    conv_back(HEADS // 2, d_b * b_slope)
    conv_back(HEADS // 2 + 1, d_c * c_slope)
    heads = mm(sums[...], spread_mat[:LANES, :], ((1,), (1,)))
    d_step = heads[2 * BLOCK : 3 * BLOCK] + heads[3 * BLOCK : 4 * BLOCK]
    d_running = heads[:BLOCK] + heads[BLOCK : 2 * BLOCK]
    d_end = heads[4 * BLOCK : 4 * BLOCK + 1] + heads[4 * BLOCK + 16 : 4 * BLOCK + 17]
    upper = (col >= row).astype(f32)
    d_decay = d_end + lax.dot_general(
        upper, d_running, (((1,), (0,)), ((), ())), precision=highest, preferred_element_type=f32
    )
    d_raw = (d_step + d_decay * rate) * sigmoid(pre)
    raw_sum, log_sum = total(d_raw), total(d_decay * rate * step)
    for shard in range(2):
        dp_ref[shard, 50:51, :] += raw_sum
        dp_ref[shard, 51:52, :] += log_sum
    rawg_all[here, :] = d_raw.astype(bf16)


class Reduction:
    def __init__(self, plan, m, bufs, sems):
        self.plan, self.m, self.bufs = plan, m, bufs
        self.send_sem, self.recv_sem, self.zs_sem, self.zr_sem, self.out_sem = sems
        s, r, flip = exchange_ids()
        self.s, self.r = s, r
        self.core, self.xbit, self.zed = lax.rem(r, 2), lax.rem(lax.div(r, 2), 2), lax.div(r, 4)
        self.y_peer, self.x_peer, self.c_peer = (1 - s, r), (s, flip(2)), (s, flip(1))

    def z_peer(self, d):
        return (self.s, lax.rem(self.zed + d, self.m) * 4 + lax.rem(self.r, 4))

    def peers(self):
        return (self.y_peer, self.x_peer, self.c_peer) + tuple(self.z_peer(d) for d in range(1, self.m))

    def geometry(self, k):
        which, start, size = self.plan[k]
        half, fourth, part = size // 2, size // 4, size // (4 * self.m)
        tile = 8 if self.bufs[which]["rc"].dtype == f32 else 16
        span = lambda at, rows: pl.ds(pl.multiple_of(at, tile), rows)
        mine = start + self.core * half
        mine_x = mine + self.xbit * fourth
        return which, start, half, fourth, part, span, mine, mine_x

    def local(self, k):
        which, start, half, fourth, part, span, mine, mine_x = self.geometry(k)
        b = self.bufs[which]
        return pltpu.make_async_copy(
            b["src"].at[:, span(mine, half)], b["loc"].at[:, pl.ds(start // 2, half)], self.out_sem.at[0, k]
        )

    def give(self, k):
        which, start, half = self.geometry(k)[:3]
        b = self.bufs[which]
        rows = pl.ds(start, 2 * half)
        return pltpu.make_async_copy(b["out"].at[rows], b["dst"].at[rows], self.out_sem.at[1, k])

    def copies(self, k, step):
        which, start, half, fourth, part, span, mine, mine_x = self.geometry(k)
        b = self.bufs[which]
        m, zed = self.m, self.zed

        def one(src, dst, lane, peer):
            return [
                pltpu.make_async_remote_copy(
                    src, dst, self.send_sem.at[lane, k], self.recv_sem.at[lane, k], device_id=peer,
                    device_id_type=MESH,
                )
            ]

        y_rows = pl.ds(start // 2, half)
        if step == 0:
            return one(
                b["src"].at[:, span(start + (1 - self.core) * half, half)], b["rc"].at[:, y_rows], 0, self.c_peer
            )
        if step == 1:
            return one(b["rc"].at[1 - self.s, y_rows], b["ry"].at[y_rows], 1, self.y_peer)
        if step == 2:
            away = span(start // 2 + (1 - self.xbit) * fourth, fourth)
            return one(b["ry"].at[away], b["rx"].at[pl.ds(start // 4, fourth)], 2, self.x_peer)
        if step in (3, 4):
            found = []
            for d in range(1, m):
                if step == 3:
                    there = lax.rem(zed + d, m)
                    src = b["rx"].at[span(start // 4 + there * part, part)]
                    dst = b["rz"].at[d - 1, pl.ds(start // (4 * m), part)]
                else:
                    src = dst = b["out"].at[span(mine_x + zed * part, part)]
                found.append(
                    pltpu.make_async_remote_copy(
                        src, dst, self.zs_sem.at[step - 3, k, d - 1], self.zr_sem.at[step - 3, k, d - 1],
                        device_id=self.z_peer(d), device_id_type=MESH,
                    )
                )
            return found
        rows = span(mine_x, fourth) if step == 5 else span(mine, half)
        return one(b["out"].at[rows], b["out"].at[rows], step - 2, self.x_peer if step == 5 else self.c_peer)

    def add(self, k, step):
        which, start, half, fourth, part, span, mine, mine_x = self.geometry(k)
        b = self.bufs[which]
        kind = b["rc"].dtype
        f = lambda v: v.astype(f32)
        y_rows = pl.ds(start // 2, half)
        x_rows = pl.ds(start // 4, fourth)
        if step == 1:
            if "loc" in b:
                self.local(k).wait()
                mine_part = b["loc"][:, y_rows]
            else:
                mine_part = b["src"][:, span(mine, half)]
            b["rc"][:, y_rows] = (f(b["rc"][:, y_rows]) + f(mine_part)).astype(kind)
        elif step == 2:
            b["ry"][y_rows] = (f(b["ry"][y_rows]) + f(b["rc"][self.s, y_rows])).astype(kind)
        elif step == 3:
            kept = b["ry"][span(start // 2 + self.xbit * fourth, fourth)]
            b["rx"][x_rows] = (f(b["rx"][x_rows]) + f(kept)).astype(kind)
        elif step == 4:
            result = f(b["rx"][span(start // 4 + self.zed * part, part)])
            for d in range(1, self.m):
                result = result + f(b["rz"][d - 1, pl.ds(start // (4 * self.m), part)])
            b["out"][span(mine_x + self.zed * part, part)] = result.astype(kind)

    def stage(self, k, step):
        if step == 0 and "loc" in self.bufs[self.plan[k][0]]:
            self.local(k).start()
        if step > 0:
            for copy in self.copies(k, step - 1):
                copy.wait_recv()
        self.add(k, step)
        if step < 7:
            for copy in self.copies(k, step):
                copy.start()
        else:
            self.give(k).start()

    def finish(self):
        for k in range(len(self.plan)):
            for step in range(7):
                for copy in self.copies(k, step):
                    copy.wait_send()
            self.give(k).wait()


def back_kernel(
    plan, begin, m, blocks,
    aux_ref, p_ref, spread_ref, ci_ref, conv_ref, raw_ref, run_ref, y_ref, dy_ref, state_ref,
    u_ref, g_ref, zg_ref, dgate_ref, normed_hbm, g_hbm, c_hbm, d_hbm, outg_hbm, gateg_hbm,
    ingrad_ref, out_sum, gate_sum, conv_sum, small_sum,
    zx_all, rawg_all, dp_ref, buf, d_hidden, wide, d_left, entered, left, sums,
    normed_all, g_all, c_all, d_all, conv_x, small_x, *rest,
):
    step_at = pl.program_id(0)
    steps = pl.num_programs(0)
    names = (("loc", "rc", "ry", "rx", "rz", "out"), ("rc", "ry", "rx", "rz", "out"))
    sources = (
        (outg_hbm, out_sum, names[0]), (gateg_hbm, gate_sum, names[0]),
        (conv_x, conv_sum, names[1]), (small_x, small_sum, names[1]),
    )
    bufs, at = [], 0
    for src, dst, held in sources:
        bufs.append(dict(zip(held, rest[at : at + len(held)]), src=src, dst=dst))
        at += len(held)
    load_sem = rest[-1]
    work = Reduction(plan, m, bufs, rest[at:-1])
    loads = [
        pltpu.make_async_copy(src, dst, load_sem.at[i])
        for i, (src, dst) in enumerate(
            ((normed_hbm, normed_all), (g_hbm, g_all), (c_hbm, c_all), (d_hbm, d_all))
        )
    ]

    def tick(t):
        for k in range(len(plan)):
            if 0 <= t - begin[k] < 8:
                work.stage(k, t - begin[k])

    @pl.when(step_at == 0)
    def _():
        meet(work.peers())
        buf[BLOCK:, :] = jnp.zeros((8, XBC), f32)
        d_hidden[...] = jnp.zeros_like(d_hidden)
        dp_ref[...] = jnp.zeros_like(dp_ref)
        dp_ref[:, 44:50, :] = dgate_ref[:, :6, :]

    for t in range(blocks):
        @pl.when(step_at == t)
        def _():
            tick(t)
            if t == 0:
                for load in loads:
                    load.start()

    @pl.when(step_at < blocks)
    def _():
        here = pl.ds(pl.multiple_of((blocks - 1 - step_at) * BLOCK, BLOCK), BLOCK)
        scan_back_step(
            here, aux_ref, p_ref, spread_ref, ci_ref, conv_ref, raw_ref, run_ref, y_ref, dy_ref, state_ref,
            zx_all, rawg_all, dp_ref, buf, d_hidden, wide, d_left, entered, left, sums,
        )

    size = u_ref.shape[0]
    half = normed_all.shape[1] // 2
    parts = [c for c in plan if c[0] == 2]
    count = zx_all.shape[0] // size
    for j in range(count):
        @pl.when(step_at == blocks + j)
        def _():
            if j == 0:
                for load in loads:
                    load.wait()
                if conv_x.shape[1] > XBC:
                    conv_x[:, XBC:] = jnp.zeros((2, conv_x.shape[1] - XBC, half), bf16)
                normed = normed_all[...]
                step_grad = mm(jnp.transpose(rawg_all[...])[:HEADS], normed)
                if small_x.shape[1] > LANES:
                    small_x[:, LANES:] = jnp.zeros((2, small_x.shape[1] - LANES, LANES), f32)
                for i in range(2):
                    for piece in range(half // LANES):
                        at = i * half + piece * LANES
                        row = 56 + piece * HEADS
                        small_x[i, row : row + HEADS, :] = step_grad[:, at : at + LANES]
            for which, start, rows in parts[j :: count]:
                for at in range(start, min(start + rows, XBC), 256):
                    turned = jnp.transpose(zx_all[:, at : at + 256])
                    grad = mm(turned, normed_all[...]).astype(bf16)
                    for i in range(2):
                        conv_x[i, at : at + 256, :] = grad[:, i * half : (i + 1) * half]
            if j < count - 1:
                tick(blocks + j)
            here = pl.ds(j * size, size)
            zg, zc, rg = zg_ref[...], zx_all[here, :], rawg_all[here, : d_all.shape[1]]
            grad = jnp.concatenate(
                [mm(zg, g_all[i]) + mm(zc, c_all[i]) + mm(rg, d_all[i]) for i in range(2)], axis=1
            )
            p = p_ref[...].astype(f32)
            u = u_ref[...].astype(f32)
            inv = lax.rsqrt(jnp.mean(u * u, axis=-1, keepdims=True) + eps)
            gain_sum = total(grad * u * inv)
            for i in range(2):
                for piece in range(half // LANES):
                    at = i * half + piece * LANES
                    dp_ref[i, piece : piece + 1, :] += gain_sum[:, at : at + LANES]
            lifted = grad * gain_row(p)
            mean_u = jnp.mean(lifted * u, axis=-1, keepdims=True)
            ingrad_ref[...] = (
                g_ref[...].astype(f32) + inv * lifted - u * (inv * inv * inv * mean_u)
            ).astype(bf16)
            if j == count - 1:
                small_x[:, :56, :] = dp_ref[...]
                for t in range(blocks + j, max(begin) + 8):
                    tick(t)
                work.finish()


def full(a):
    return pl.BlockSpec(a.shape, lambda i: (0,) * a.ndim, pipeline_mode=pl.Buffered(1))


def compute_params(mib=56):
    return pltpu.CompilerParams(
        dimension_semantics=("arbitrary",), vmem_limit_bytes=mib * 1024 * 1024
    )


def segment_rows(segment):
    tokens = segment.shape[0]
    blocks = tokens // BLOCK
    shifted = [jnp.pad(segment, (k, 0), constant_values=-1)[:tokens] for k in range(CONV)]
    after = [jnp.pad(segment, (0, k), constant_values=-1)[k:] for k in range(CONV)]
    by_block = segment.reshape(blocks, BLOCK)
    before = jnp.pad(by_block[:-1, -1], (1, 0), constant_values=-1)
    flat = lambda v: v.reshape(blocks, BLOCK)
    rows = (
        [flat(shifted[k] == segment) for k in (1, 2, 3)]
        + [by_block == before[:, None], by_block == by_block[:, -1:], by_block]
        + [flat(after[k] == segment) for k in (1, 2, 3)]
    )
    rows = rows + [by_block] * (16 - len(rows))
    return jnp.stack([r.astype(f32) for r in rows], axis=1)


def spread_matrix():
    owner = jnp.arange(INNER) // HEADDIM
    one = (jnp.arange(LANES)[:, None] == owner[None, :]).astype(bf16)
    return jnp.concatenate([one, one], axis=0)


def rows_of(size, cols, order):
    return pl.BlockSpec((size, cols), lambda i: (order(i), 0))


shape = jax.ShapeDtypeStruct
fwd = lambda i: i


def acc(rows):
    return pl.BlockSpec((2, rows, LANES), lambda i: (0, 0, 0))


def scan_forward(layer_in, aux, c_all, d_all, pack, spread_mat):
    tokens, width = layer_in.shape
    blocks = tokens // BLOCK
    rows = lambda cols: rows_of(BLOCK, cols, fwd)
    return pl.pallas_call(
        k1_kernel,
        grid=(blocks,),
        in_specs=[
            rows(width), pl.BlockSpec((1, 16, BLOCK), lambda i: (i, 0, 0)), full(c_all), full(d_all),
            full(pack), full(spread_mat),
        ],
        out_specs=[
            rows(width), rows(XBC), rows(XBC), rows(LANES), rows(LANES), rows(INNER),
            pl.BlockSpec((1, STATE, INNER), lambda i: (i, 0, 0)),
        ],
        out_shape=[
            shape((tokens, width), bf16), shape((tokens, XBC), bf16), shape((tokens, XBC), f32),
            shape((tokens, LANES), f32), shape((tokens, LANES), f32), shape((tokens, INNER), f32),
            shape((blocks, STATE, INNER), bf16),
        ],
        scratch_shapes=[
            pltpu.VMEM((BLOCK + 8, XBC), f32), pltpu.VMEM((STATE, INNER), f32),
            pltpu.VMEM((3 * BLOCK, INNER), f32), pltpu.VMEM((BLOCK, INNER), f32),
        ],
        compiler_params=compute_params(),
        cost_estimate=pl.CostEstimate(
            flops=2 * tokens * width * XBC * 4, bytes_accessed=30_000_000, transcendentals=tokens * 5000
        ),
        name="scan_forward",
    )(layer_in, aux, c_all, d_all, pack, spread_mat)


def gate_both(layer_in, normed, cotangent, y, g_all, o_all, pack):
    tokens, width = layer_in.shape
    size = 256
    rows = lambda cols: rows_of(size, cols, fwd)
    return pl.pallas_call(
        k2_kernel,
        grid=(tokens // size,),
        in_specs=[
            rows(width), rows(width), rows(width), rows(INNER), full(g_all), full(o_all), full(pack),
        ],
        out_specs=[rows(width), rows(INNER), rows(INNER), rows(INNER), acc(8)],
        out_shape=[
            shape((tokens, width), bf16), shape((tokens, INNER), bf16), shape((tokens, INNER), f32),
            shape((tokens, INNER), bf16), shape((2, 8, LANES), f32),
        ],
        scratch_shapes=[pltpu.VMEM((size, INNER), f32)] * 4,
        compiler_params=compute_params(),
        cost_estimate=pl.CostEstimate(
            flops=2 * tokens * width * INNER * 4, bytes_accessed=30_000_000, transcendentals=tokens * 5000
        ),
        name="gate_both",
    )(layer_in, normed, cotangent, y, g_all, o_all, pack)


def backward(
    layer_in, cotangent, aux, pack, spread_mat, ci, conv, raw, running, y, dy, states, zx_gate, d_gate, normed,
    g_all, c_all, d_all, out_grad, gate_grad,
):
    tokens, width = layer_in.shape
    blocks = tokens // BLOCK
    size = 256
    late = tokens // size
    half = width // 2
    m = lax.axis_size("rep") // 4

    def padded(rows, kind):
        unit = (16 if kind == bf16 else 8) * 4 * m
        return -(-rows // unit) * unit

    arrays = (
        (padded(out_grad.shape[1], bf16), width, bf16, 3, True), (padded(INNER, bf16), half, bf16, 3, True),
        (padded(XBC, bf16), half, bf16, late, False), (padded(LANES, f32), LANES, f32, 1, False),
    )
    plan, begin = [], []
    first = (0, 3, blocks, blocks + late - 1)
    for which, (n, _, kind, pieces, _) in enumerate(arrays):
        units = n // ((16 if kind == bf16 else 8) * 4 * m)
        pieces = min(pieces, units)
        edges = [-(-units * i // pieces) * (n // units) for i in range(pieces + 1)]
        for i in range(pieces):
            plan.append((which, edges[i], edges[i + 1] - edges[i]))
            begin.append(first[which] + i)
    grow = lambda a, n: jnp.pad(a, ((0, 0), (0, n - a.shape[1]), (0, 0)))
    out_grad, gate_grad = grow(out_grad, arrays[0][0]), grow(gate_grad, arrays[1][0])
    scratch = []
    for n, c, kind, _, far in arrays:
        if far:
            scratch.append(pltpu.VMEM((2, n // 2, c), kind))
        scratch += [
            pltpu.VMEM((2, n // 2, c), kind), pltpu.VMEM((n // 2, c), kind), pltpu.VMEM((n // 4, c), kind),
            pltpu.VMEM((max(m - 1, 1), n // (4 * m), c), kind), pltpu.VMEM((n, c), kind),
        ]
    chunks = len(plan)
    dma = pltpu.SemaphoreType.DMA
    back = lambda i: jnp.maximum(blocks - 1 - i, 0)
    row = lambda i: jnp.maximum(i - blocks, 0)
    rows = lambda cols: rows_of(BLOCK, cols, back)
    late_rows = lambda cols: rows_of(size, cols, row)
    far_spec = pl.BlockSpec(memory_space=pl.ANY)
    vm = pltpu.VMEM
    return pl.pallas_call(
        functools.partial(back_kernel, tuple(plan), tuple(begin), m, blocks),
        grid=(blocks + late,),
        in_specs=[
            pl.BlockSpec((1, 16, BLOCK), lambda i: (back(i), 0, 0)), full(pack), full(spread_mat),
            rows(XBC), rows(XBC), rows(LANES), rows(LANES), rows(INNER), rows(INNER),
            pl.BlockSpec((1, STATE, INNER), lambda i: (back(i), 0, 0)),
            late_rows(width), late_rows(width), late_rows(INNER), full(d_gate),
        ]
        + [far_spec] * 6,
        out_specs=[late_rows(width)] + [far_spec] * 4,
        out_shape=[shape((tokens, width), bf16)] + [shape((n, c), kind) for n, c, kind, _, _ in arrays],
        scratch_shapes=[
            vm((tokens, XBC), bf16), vm((tokens, LANES), bf16), vm((2, 56, LANES), f32),
            vm((BLOCK + 8, XBC), f32), vm((STATE, INNER), f32), vm((3 * BLOCK, INNER), f32),
            vm((BLOCK, INNER), f32), vm((BLOCK, INNER), bf16), vm((BLOCK, INNER), bf16),
            vm((4 * BLOCK + 32, INNER), bf16),
            vm(normed.shape, bf16), vm(g_all.shape, bf16), vm(c_all.shape, bf16), vm(d_all.shape, bf16),
            vm((2, arrays[2][0], half), bf16), vm((2, arrays[3][0], LANES), f32),
        ]
        + scratch
        + [
            dma((5, chunks)), dma((5, chunks)), dma((2, chunks, max(m - 1, 1))),
            dma((2, chunks, max(m - 1, 1))), dma((2, chunks)), dma((4,)),
        ],
        compiler_params=pltpu.CompilerParams(
            dimension_semantics=("arbitrary",), vmem_limit_bytes=62 * 1024 * 1024, collective_id=1,
            has_side_effects=True,
        ),
        cost_estimate=pl.CostEstimate(
            flops=2 * tokens * 768 * XBC * 8, bytes_accessed=40_000_000, transcendentals=tokens * 5000
        ),
        name="backward_reduce",
    )(aux, pack, spread_mat, ci, conv, raw, running, y, dy, states, layer_in, cotangent, zx_gate, d_gate,
      normed, g_all, c_all, d_all, out_grad, gate_grad)


def pack_rows(norm_gain, conv_weight, conv_bias, dt_bias, a_log, skip_gain, gate_gain):
    lanes = lambda v: v.reshape(-1, LANES)
    own = dt_bias.size
    where = lax.axis_index("shard") * own

    def placed(v):
        return lax.dynamic_update_slice(jnp.zeros((LANES,), v.dtype), v, (where,)).reshape(1, LANES)

    rows = jnp.concatenate(
        [
            lanes(norm_gain), lanes(conv_weight), lanes(conv_bias), lanes(jnp.repeat(skip_gain, HEADDIM)),
            lanes(gate_gain), placed(dt_bias), placed(a_log),
        ],
        axis=0,
    )
    return jnp.pad(rows, ((0, 64 - rows.shape[0]), (0, 0)))


def body(
    layer_in, segment_ids, cotangent, norm_gain, in_weight, conv_weight, conv_bias, dt_bias, a_log,
    skip_gain, gate_gain, out_weight,
):
    width = layer_in.shape[1]
    w_t = in_weight.T
    pack = pack_rows(norm_gain, conv_weight, conv_bias, dt_bias, a_log, skip_gain, gate_gain)
    step_t = jnp.pad(w_t[WIDE:], ((0, 8), (0, 0)))
    c_all, g_all, o_all, d_all, p_all = gather(w_t, out_weight, step_t, pack)
    aux = segment_rows(segment_ids.reshape(-1))
    spread_mat = spread_matrix()
    normed, ci, conv, raw, running, y, states = scan_forward(layer_in, aux, c_all, d_all, p_all, spread_mat)
    layer_out, mixed, dy, zx_gate, d_gate = gate_both(layer_in, normed, cotangent, y, g_all, o_all, p_all)
    nt = ((0,), (0,))
    half = width // 2
    by_half = lambda a: jnp.stack([mm(a, normed[:, i * half : (i + 1) * half], nt) for i in range(2)])
    out_grad = mm(mixed, cotangent, nt).astype(bf16).reshape(2, -1, width)
    gate_grad = by_half(zx_gate).astype(bf16)
    input_grad, out_sum, gate_sum, conv_sum, small_sum = backward(
        layer_in, cotangent, aux, p_all, spread_mat, ci, conv, raw, running, y, dy, states, zx_gate, d_gate,
        normed, g_all, c_all, d_all, out_grad, gate_grad,
    )
    factor = 1.0 / (lax.axis_size("shard") * lax.axis_size("rep"))
    small_sum = small_sum * factor
    pieces = half // LANES
    step_sum = small_sum[56 : 56 + pieces * HEADS].reshape(pieces, HEADS, LANES).transpose(1, 0, 2).reshape(HEADS, half)
    in_weight_grad = jnp.concatenate(
        [gate_sum[:INNER].astype(f32) * factor, conv_sum[:XBC].astype(f32) * factor, step_sum], axis=0
    ).T
    own = dt_bias.size
    head = lambda k: lax.dynamic_slice(small_sum[50 + k], (lax.axis_index("shard") * own,), (own,))
    return (
        layer_out, input_grad, small_sum[0:3].reshape(norm_gain.shape), in_weight_grad,
        small_sum[3:31].reshape(conv_weight.shape), small_sum[31:38].reshape(conv_bias.shape),
        head(0), head(1), small_sum[38:44].reshape(own, HEADDIM).sum(axis=1),
        small_sum[44:50].reshape(gate_gain.shape), out_sum[: out_weight.shape[0]].astype(f32) * factor,
    )


def solution(mesh):
    both, shard = P(("shard", "rep"), None), P("shard")
    in_specs = (
        both, both, both, shard, P("shard", None), P(None, "shard"), shard, shard, shard, shard, shard,
        P("shard", None),
    )
    out_specs = (
        both, both, shard, P("shard", None), P(None, "shard"), shard, shard, shard, shard, shard,
        P("shard", None),
    )
    return jax.shard_map(body, mesh=mesh, in_specs=in_specs, out_specs=out_specs, check_vma=False)
```

```python
import functools

import jax
import jax.numpy as jnp
from jax import lax
from jax.experimental import pallas as pl
from jax.experimental.pallas import tpu as pltpu
from jax.sharding import PartitionSpec as P

HEADS = 24
HEADDIM = 64
STATE = 128
CONV = 4
BLOCK = 128
INNER = 1536
XBC = 1792
WIDE = INNER + XBC
LANES = 128
LOG2E = 1.4426950408889634

MESH = pl.DeviceIdType.MESH
eps = 1e-05
highest = lax.Precision.HIGHEST
f32 = jnp.float32
bf16 = jnp.bfloat16


def mm(a, b, contract=((1,), (0,))):
    return lax.dot_general(a, b, (contract, ((), ())), preferred_element_type=f32)


def mm_t(a, w_ref):
    half = w_ref.shape[2]
    nt = ((1,), (1,))
    return mm(a[:, :half], w_ref[0], nt) + mm(a[:, half:], w_ref[1], nt)


def total(v):
    return jnp.sum(v, axis=0, keepdims=True)


def sigmoid(v):
    return 0.5 + 0.5 * jnp.tanh(0.5 * v)


def softplus(v):
    small = jnp.exp(-jnp.abs(v))
    series = small * (1.0 - small * (0.5 - small * (1.0 / 3.0 - small * 0.25)))
    return jnp.maximum(v, 0.0) + jnp.where(small < 0.03, series, jnp.log(1.0 + small))


def spread(per_head, spread_mat):
    high = per_head.astype(bf16)
    rest = (per_head - high.astype(f32)).astype(bf16)
    return mm(jnp.concatenate([high, rest], axis=1), spread_mat)


def gain_row(p):
    return jnp.concatenate([p[i, j : j + 1, :] for i in range(2) for j in range(3)], axis=1)


def conv_tap(p, tap, j):
    at = 3 + tap * 7 + j % 7
    return p[j // 7, at : at + 1, :]


def conv_bias(p, j):
    return p[j // 7, 31 + j % 7 : 32 + j % 7, :]


def gate_row(p, pair):
    return p[pair // 6, 38 + pair % 6 : 39 + pair % 6, :]


def head_rows(p):
    return p[0, 40:48, :] + pltpu.roll(p[1, 40:48, :], HEADS // 2, 1)


def fill_spread(ref):
    row = lax.broadcasted_iota(jnp.int32, ref.shape, 0) & (LANES - 1)
    col = lax.broadcasted_iota(jnp.int32, ref.shape, 1)
    ref[...] = jnp.where(row == lax.shift_right_logical(col, 6), 1.0, 0.0).astype(bf16)


def lane_pair(values, first):
    lane = lax.broadcasted_iota(jnp.int32, values.shape, 1)
    zero = jnp.zeros_like(values)
    return jnp.concatenate(
        [jnp.where(lane < HEADDIM, values, zero), jnp.where(lane >= HEADDIM, values, zero)], axis=0
    )


def spread_of(running, running_t, head):
    diff = running[:, head : head + 1] - running_t[head : head + 1, :]
    return jnp.exp2(jnp.minimum(diff, 0.0))


def spread_back(running, running_t, head):
    diff = running_t[head : head + 1, :] - running[:, head : head + 1]
    return jnp.exp2(jnp.minimum(diff, 0.0))


def exchange_ids():
    s, r = lax.axis_index("shard"), lax.axis_index("rep")
    flip = lambda b: r + b - 2 * b * (lax.rem(lax.div(r, b), 2))
    return s, r, flip


def meet(peers):
    barrier = pltpu.get_barrier_semaphore()
    for peer in peers:
        pl.semaphore_signal(barrier, inc=1, device_id=peer, device_id_type=MESH)
    pl.semaphore_wait(barrier, len(peers))


def scan_forward_step(
    u_ref, aux_ref, c_ref, d_ref, p_ref, spread_ref, normed_ref, ci_ref, conv_ref, raw_ref, run_ref, y_ref,
    state_ref, buf, hidden, wide, inter,
):
    p = p_ref[...].astype(f32)
    heads_at = head_rows(p)
    u = u_ref[...].astype(f32)
    inv = lax.rsqrt(jnp.mean(u * u, axis=-1, keepdims=True) + eps)
    normed = (u * inv * gain_row(p)).astype(bf16)
    normed_ref[...] = normed
    buf[8 : 8 + BLOCK, :] = mm_t(normed, c_ref)
    half = normed.shape[1] // 2
    raw = sum(mm(normed[:, i * half : (i + 1) * half], d_ref[i].astype(bf16), ((1,), (1,))) for i in range(2))
    raw_ref[:, : raw.shape[1]] = raw
    raw_ref[:, raw.shape[1] :] = jnp.zeros((BLOCK, LANES - raw.shape[1]), f32)
    aux = jnp.transpose(aux_ref[0])
    masks = [jnp.broadcast_to(aux[:, k : k + 1], (BLOCK, LANES)) for k in range(3)]
    step = softplus(raw_ref[...] + heads_at[4:5, :])
    decay = (-LOG2E) * jnp.exp(heads_at[5:6, :]) * step
    row = lax.broadcasted_iota(jnp.int32, (BLOCK, BLOCK), 0)
    col = lax.broadcasted_iota(jnp.int32, (BLOCK, BLOCK), 1)
    lower = (row >= col).astype(f32)
    running = lax.dot_general(
        lower, decay, (((1,), (0,)), ((), ())), precision=highest, preferred_element_type=f32
    )
    run_ref[...] = running
    running_t = jnp.transpose(running)
    entering = jnp.exp2(running) * aux[:, 3:4]
    leaving = jnp.exp2(running[BLOCK - 1 : BLOCK, :] - running) * aux[:, 4:5]
    wide[...] = spread(jnp.concatenate([step, entering, leaving, heads_at], axis=0), spread_ref[...])

    def conv_chunk(j):
        cols = slice(j * LANES, (j + 1) * LANES)
        x = buf[8 : 8 + BLOCK, cols]
        ci_ref[:, cols] = x.astype(bf16)
        conv = conv_bias(p, j) + conv_tap(p, CONV - 1, j) * x
        for k in range(1, CONV):
            conv = conv + conv_tap(p, CONV - 1 - k, j) * (buf[8 - k : 8 - k + BLOCK, cols] * masks[k - 1])
        conv_ref[:, cols] = conv
        return conv * sigmoid(conv)

    b_low = conv_chunk(HEADS // 2).astype(bf16)
    c_low = conv_chunk(HEADS // 2 + 1).astype(bf16)
    b_t = jnp.transpose(b_low)
    allowed = (row >= col) & (aux[:, 5:6] == aux_ref[0, 5:6, :])
    scores = jnp.where(allowed, mm(c_low, b_low, ((1,), (1,))), 0.0)
    state_low = hidden[...].astype(bf16)
    state_ref[0] = state_low
    inter[...] = mm(c_low, state_low)
    for pair in range(HEADS // 2):
        cols = slice(pair * LANES, (pair + 1) * LANES)
        values = conv_chunk(pair)
        weighted = values * wide[0:BLOCK, cols]
        first = (spread_of(running, running_t, 2 * pair) * scores).astype(bf16)
        second = (spread_of(running, running_t, 2 * pair + 1) * scores).astype(bf16)
        enter = wide[BLOCK : 2 * BLOCK, cols]
        y_ref[:, cols] = (
            mm(jnp.concatenate([first, second], axis=1), lane_pair(weighted.astype(bf16), pair))
            + inter[:, cols] * enter
            + wide[3 * BLOCK + 6 : 3 * BLOCK + 7, cols] * values
        )
        left = (weighted * wide[2 * BLOCK : 3 * BLOCK, cols]).astype(bf16)
        hidden[:, cols] = hidden[:, cols] * wide[2 * BLOCK - 1 : 2 * BLOCK, cols] + mm(b_t, left)
    buf[0:8, :] = buf[BLOCK : BLOCK + 8, :]


def segment_masks(seg, aux_all):
    blocks = seg.shape[0]
    block = lax.broadcasted_iota(jnp.int32, seg.shape, 0)
    lane = lax.broadcasted_iota(jnp.int32, seg.shape, 1)
    last = jnp.sum(jnp.where(lane == LANES - 1, seg, 0.0), axis=1, keepdims=True)
    last = jnp.broadcast_to(last, seg.shape)
    before = jnp.where(block == 0, -1.0, pltpu.roll(seg, 1, 0))
    after = jnp.where(block == blocks - 1, -1.0, pltpu.roll(seg, blocks - 1, 0))
    rows = []
    for k in range(1, CONV):
        other = jnp.where(lane >= k, pltpu.roll(seg, k, 1), pltpu.roll(before, k, 1))
        rows.append(other == seg)
    rows.append(jnp.where(block == 0, -1.0, pltpu.roll(last, 1, 0)) == seg)
    rows.append(last == seg)
    rows.append(seg)
    for k in range(1, CONV):
        other = jnp.where(lane < LANES - k, pltpu.roll(seg, LANES - k, 1), pltpu.roll(after, LANES - k, 1))
        rows.append(other == seg)
    aux_all[...] = jnp.zeros_like(aux_all)
    for at, value in enumerate(rows):
        value = value if value.dtype == f32 else jnp.where(value, 1.0, 0.0)
        for b in range(blocks):
            aux_all[b, at : at + 1, :] = value[b : b + 1, :]


class Gather:
    def __init__(self, pieces, sections, send_sem, recv_sem):
        s, r, flip = exchange_ids()
        self.s, self.pieces, self.sections = s, pieces, sections
        self.send_sem, self.recv_sem = send_sem, recv_sem
        self.y_peer, self.x_peer, self.c_peer = (1 - s, r), (s, flip(2)), (s, flip(1))
        self.quarter, self.x_quarter = lax.rem(r, 4), lax.rem(flip(2), 4)
        self.todo = [(which, piece) for which, (_, count) in enumerate(pieces) for piece in range(count)]

    def rows_at(self, which, part, piece, base=0):
        size, count = self.pieces[which]
        return pl.ds(pl.multiple_of(base + (part * count + piece) * size, 16), size)

    def copy(self, k, lane):
        which, piece = self.todo[k]
        src, base, dst = self.sections[which]
        if lane == 0:
            block = src.at[self.rows_at(which, self.quarter, piece, base)]
            there = dst.at[self.s, self.rows_at(which, self.quarter, piece)]
        else:
            part = self.x_quarter if lane == 3 else self.quarter
            block = there = dst.at[1 - self.s, self.rows_at(which, part, piece)]
        return pltpu.make_async_remote_copy(
            block, there, self.send_sem.at[lane, k], self.recv_sem.at[lane, k],
            device_id=(self.y_peer, self.x_peer, self.c_peer, self.c_peer)[lane], device_id_type=MESH,
        )

    def near(self, k):
        self.copy(k, 0).wait_recv()
        self.copy(k, 1).start()
        self.copy(k, 2).start()

    def far(self, k):
        self.copy(k, 1).wait_recv()
        self.copy(k, 3).start()

    def finish(self, ks):
        for k in ks:
            for lane in (2, 3):
                self.copy(k, lane).wait_recv()

    def sent(self):
        for k in range(len(self.todo)):
            for lane in range(4):
                self.copy(k, lane).wait_send()


def front_kernel(
    pieces, blocks,
    u_ref, seg_ref, w_hbm, o_hbm, d_hbm, p_hbm,
    normed_ref, ci_ref, conv_ref, raw_ref, run_ref, y_ref, state_ref, aux_out, c_out, g_all, o_all, d_out, p_out,
    buf, hidden, wide, inter, spread_ref, c_all, d_all, p_all, g_stage, o_stage, aux_all,
    local_sem, small_sem, send_sem, recv_sem,
):
    step_at = pl.program_id(0)
    sections = ((w_hbm, INNER, c_all), (w_hbm, 0, g_all), (o_hbm, 0, o_all))
    work = Gather(pieces, sections, send_sem, recv_sem)
    s = work.s
    urgent = range(pieces[0][1])
    later = range(pieces[0][1], len(work.todo))
    small = [
        pltpu.make_async_remote_copy(
            src, dst.at[s], small_sem.at[0, i], small_sem.at[1, i], device_id=work.y_peer, device_id_type=MESH
        )
        for i, (src, dst) in enumerate(((d_hbm, d_all), (p_hbm, p_all)))
    ]
    own = [
        pltpu.make_async_copy(src, dst, local_sem.at[i])
        for i, (src, dst) in enumerate(
            (
                (d_hbm, d_all.at[s]), (p_hbm, p_all.at[s]), (w_hbm.at[pl.ds(INNER, XBC)], c_all.at[s]),
                (w_hbm.at[pl.ds(0, INNER)], g_stage), (o_hbm, o_stage),
            )
        )
    ]
    back = [
        pltpu.make_async_copy(src, dst, local_sem.at[5 + i])
        for i, (src, dst) in enumerate(
            ((d_all, d_out), (p_all, p_out), (c_all, c_out), (g_stage, g_all.at[s]), (o_stage, o_all.at[s]))
        )
    ]

    @pl.when(step_at == 0)
    def _():
        meet((work.y_peer, work.x_peer, work.c_peer))
        for copy in small:
            copy.start()
        for k in urgent:
            work.copy(k, 0).start()
        for copy in own:
            copy.start()
        buf[0:8, :] = jnp.zeros((8, XBC), f32)
        hidden[...] = jnp.zeros_like(hidden)
        fill_spread(spread_ref)
        for k in urgent:
            work.near(k)
            if k > 0:
                work.far(k - 1)
        for k in later[:2]:
            work.copy(k, 0).start()
        work.far(urgent[-1])
        for copy in small + own[:3]:
            copy.wait()
        work.finish(urgent)
        segment_masks(seg_ref[...].astype(f32), aux_all)

    for t in range(1, blocks):
        @pl.when(step_at == t)
        def _():
            if t == 1:
                for copy in own[3:]:
                    copy.wait()
                for copy in back:
                    copy.start()
            for i, k in enumerate(later):
                if t == i - 1:
                    work.copy(k, 0).start()
                if t == 2 + i:
                    work.near(k)
                if t == 4 + i:
                    work.far(k)

    aux_out[0] = aux_all[step_at]
    scan_forward_step(
        u_ref, aux_all.at[pl.ds(step_at, 1)], c_all, d_all, p_all, spread_ref, normed_ref, ci_ref, conv_ref, raw_ref, run_ref, y_ref,
        state_ref, buf, hidden, wide, inter,
    )

    @pl.when(step_at == blocks - 1)
    def _():
        for i, k in enumerate(later):
            if i - 1 >= blocks:
                work.copy(k, 0).start()
            if 2 + i >= blocks:
                work.near(k)
        for i, k in enumerate(later):
            if 4 + i >= blocks:
                work.far(k)
        work.finish(later)
        work.sent()
        for copy in back:
            copy.wait()


def k2_kernel(
    u_ref, normed_ref, g_ref, y_ref, g_all_ref, o_ref, p_ref,
    out_ref, mixed_ref, dy_ref, zx_ref, dgate_ref,
    gate, mixed_grad, gated, sig,
):
    rows = u_ref.shape[0]

    @pl.when(pl.program_id(0) == 0)
    def _():
        dgate_ref[...] = jnp.zeros_like(dgate_ref)

    p = p_ref[...].astype(f32)
    gate[...] = mm_t(normed_ref[...], g_all_ref)
    out_w = o_ref[...].reshape(INNER, -1)
    mixed_grad[...] = mm(g_ref[...], out_w, ((1,), (1,)))
    SUB = 64
    for sub in range(rows // SUB):
        r = slice(sub * SUB, (sub + 1) * SUB)
        square = jnp.zeros((SUB, LANES), f32)
        cross = jnp.zeros((SUB, LANES), f32)
        for pair in range(HEADS // 2):
            cols = slice(pair * LANES, (pair + 1) * LANES)
            v = gate[r, cols]
            s = sigmoid(v)
            sig[r, cols] = s
            product = y_ref[r, cols] * (v * s)
            gated[r, cols] = product
            square = square + product * product
            cross = cross + mixed_grad[r, cols] * gate_row(p, pair) * product
        inv = lax.rsqrt(jnp.sum(square, axis=-1, keepdims=True) * (1.0 / INNER) + eps)
        back = inv * inv * inv * (jnp.sum(cross, axis=-1, keepdims=True) * (1.0 / INNER))
        inv = jnp.broadcast_to(inv, (SUB, LANES))
        back = jnp.broadcast_to(back, (SUB, LANES))
        for pair in range(HEADS // 2):
            cols = slice(pair * LANES, (pair + 1) * LANES)
            v, s, product = gate[r, cols], sig[r, cols], gated[r, cols]
            scaled = product * inv
            gain = gate_row(p, pair)
            mixed_ref[r, cols] = (scaled * gain).astype(bf16)
            mg = mixed_grad[r, cols]
            dgate_ref[pair // 6, pair % 6 : pair % 6 + 1, :] += total(mg * scaled)
            d_gated = inv * (mg * gain) - product * back
            act = v * s
            dy_ref[r, cols] = d_gated * act
            zx_ref[r, cols] = (d_gated * y_ref[r, cols] * (s + act * (1.0 - s))).astype(bf16)
    out_ref[...] = (u_ref[...].astype(f32) + mm(mixed_ref[...], out_w)).astype(bf16)


def scan_back_step(
    here, aux_ref, p_ref, spread_ref, ci_ref, conv_ref, raw_ref, run_ref, y_ref, dy_ref, state_ref,
    zx_all, rawg_all, dp_ref, buf, d_hidden, wide, d_left, entered, left, sums,
):
    p = p_ref[...].astype(f32)
    heads_at = head_rows(p)
    aux = jnp.transpose(aux_ref[0])
    masks = [jnp.broadcast_to(aux[:, k : k + 1], (BLOCK, LANES)) for k in range(6, 9)]
    pre = raw_ref[...] + heads_at[4:5, :]
    step = softplus(pre)
    rate = -jnp.exp(heads_at[5:6, :])
    running = run_ref[...]
    running_t = jnp.transpose(running)
    entering = jnp.exp2(running) * aux[:, 3:4]
    leaving = jnp.exp2(running[BLOCK - 1 : BLOCK, :] - running) * aux[:, 4:5]
    spread_mat = spread_ref[...]
    wide[...] = spread(jnp.concatenate([step, entering, leaving, heads_at], axis=0), spread_mat)

    def act_chunk(j):
        cols = slice(j * LANES, (j + 1) * LANES)
        conv = conv_ref[:, cols]
        sig = sigmoid(conv)
        act = conv * sig
        return act, sig + act * (1.0 - sig)

    def conv_back(j, d_conv):
        cols = slice(j * LANES, (j + 1) * LANES)
        buf[:BLOCK, cols] = d_conv
        ci = ci_ref[:, cols].astype(f32)
        shard, at = j // 7, j % 7
        dp_ref[shard, 31 + at : 32 + at, :] += total(d_conv)
        dp_ref[shard, 24 + at : 25 + at, :] += total(ci * d_conv)
        d_in = conv_tap(p, CONV - 1, j) * d_conv
        for k in range(1, CONV):
            later = buf[k : BLOCK + k, cols] * masks[k - 1]
            d_in = d_in + conv_tap(p, CONV - 1 - k, j) * later
            row_at = 3 + (CONV - 1 - k) * 7 + at
            dp_ref[shard, row_at : row_at + 1, :] += total(ci * later)
        zx_all[here, cols] = d_in.astype(bf16)
        buf[BLOCK:, cols] = d_conv[:8, :]

    b_act, b_slope = act_chunk(HEADS // 2)
    c_act, c_slope = act_chunk(HEADS // 2 + 1)
    b_low, c_low = b_act.astype(bf16), c_act.astype(bf16)
    c_t = jnp.transpose(c_low)
    row = lax.broadcasted_iota(jnp.int32, (BLOCK, BLOCK), 0)
    col = lax.broadcasted_iota(jnp.int32, (BLOCK, BLOCK), 1)
    allowed_t = (col >= row) & (aux[:, 5:6] == aux_ref[0, 5:6, :])
    scores_t = jnp.where(allowed_t, mm(b_low, c_low, ((1,), (1,))), 0.0)
    d_state_low = d_hidden[...].astype(bf16)
    d_left[...] = mm(b_low, d_state_low)
    d_scores_t = jnp.zeros((BLOCK, BLOCK), f32)
    for pair in range(HEADS // 2):
        cols = slice(pair * LANES, (pair + 1) * LANES)
        values, slope = act_chunk(pair)
        step_wide = wide[0:BLOCK, cols]
        enter = wide[BLOCK : 2 * BLOCK, cols]
        leave = wide[2 * BLOCK : 3 * BLOCK, cols]
        dy = dy_ref[:, cols]
        skip = wide[3 * BLOCK + 6 : 3 * BLOCK + 7, cols]
        weighted = values * step_wide
        left[:, cols] = (weighted * leave).astype(bf16)
        entered_low = (dy * enter).astype(bf16)
        entered[:, cols] = entered_low
        dp_ref[pair // 6, 38 + pair % 6 : 39 + pair % 6, :] += total(dy * values)
        dy_low = dy.astype(bf16)
        w_low = weighted.astype(bf16)
        d_kernel = mm(lane_pair(w_low, pair), dy_low, ((1,), (1,)))
        spread_a = spread_back(running, running_t, 2 * pair)
        spread_b = spread_back(running, running_t, 2 * pair + 1)
        d_scores_t = d_scores_t + (d_kernel[:BLOCK] * spread_a + d_kernel[BLOCK:] * spread_b)
        kernel_two = jnp.concatenate(
            [(spread_a * scores_t).astype(bf16), (spread_b * scores_t).astype(bf16)], axis=1
        )
        d_leave = d_left[:, cols] * leave
        d_weighted = mm(kernel_two, lane_pair(dy_low, pair)) + d_leave
        w_kept = w_low.astype(f32)
        flow_in = dy_low.astype(f32) * (y_ref[:, cols] - skip * values) - w_kept * d_weighted
        flow_out = d_weighted * values
        for k, flow in enumerate((flow_in, flow_out)):
            high = flow.astype(bf16)
            sums[2 * k * BLOCK : (2 * k + 1) * BLOCK, cols] = high
            sums[(2 * k + 1) * BLOCK : (2 * k + 2) * BLOCK, cols] = (flow - high.astype(f32)).astype(bf16)
        carried = wide[2 * BLOCK - 1 : 2 * BLOCK, cols]
        d_state = d_hidden[:, cols]
        end = total(w_kept * d_leave) + total(d_state * state_ref[0, :, cols].astype(f32)) * carried
        high = end.astype(bf16)
        sums[4 * BLOCK : 4 * BLOCK + 16, cols] = jnp.broadcast_to(high, (16, LANES))
        sums[4 * BLOCK + 16 :, cols] = jnp.broadcast_to((end - high.astype(f32)).astype(bf16), (16, LANES))
        d_hidden[:, cols] = d_state * carried + mm(c_t, entered_low)
        conv_back(pair, (dy * skip + d_weighted * step_wide) * slope)
    d_scores_low = jnp.where(allowed_t, d_scores_t, 0.0).astype(bf16)
    state_low = state_ref[0]
    d_b = mm(left[...], d_state_low, ((1,), (1,))) + mm(d_scores_low, c_low)
    d_c = mm(entered[...], state_low, ((1,), (1,))) + mm(d_scores_low, b_low, ((0,), (0,)))
    conv_back(HEADS // 2, d_b * b_slope)
    conv_back(HEADS // 2 + 1, d_c * c_slope)
    heads = mm(sums[...], spread_mat[:LANES, :], ((1,), (1,)))
    d_step = heads[2 * BLOCK : 3 * BLOCK] + heads[3 * BLOCK : 4 * BLOCK]
    d_running = heads[:BLOCK] + heads[BLOCK : 2 * BLOCK]
    d_end = heads[4 * BLOCK : 4 * BLOCK + 1] + heads[4 * BLOCK + 16 : 4 * BLOCK + 17]
    upper = (col >= row).astype(f32)
    d_decay = d_end + lax.dot_general(
        upper, d_running, (((1,), (0,)), ((), ())), precision=highest, preferred_element_type=f32
    )
    d_raw = (d_step + d_decay * rate) * sigmoid(pre)
    raw_sum, log_sum = total(d_raw), total(d_decay * rate * step)
    for shard in range(2):
        dp_ref[shard, 50:51, :] += raw_sum
        dp_ref[shard, 51:52, :] += log_sum
    rawg_all[here, :] = d_raw.astype(bf16)


class Reduction:
    def __init__(self, plan, m, bufs, sems):
        self.plan, self.m, self.bufs = plan, m, bufs
        self.send_sem, self.recv_sem, self.zs_sem, self.zr_sem, self.out_sem = sems
        s, r, flip = exchange_ids()
        self.s, self.r = s, r
        self.core, self.xbit, self.zed = lax.rem(r, 2), lax.rem(lax.div(r, 2), 2), lax.div(r, 4)
        self.y_peer, self.x_peer, self.c_peer = (1 - s, r), (s, flip(2)), (s, flip(1))

    def z_peer(self, d):
        return (self.s, lax.rem(self.zed + d, self.m) * 4 + lax.rem(self.r, 4))

    def peers(self):
        return (self.y_peer, self.x_peer, self.c_peer) + tuple(self.z_peer(d) for d in range(1, self.m))

    def geometry(self, k):
        which, start, size = self.plan[k]
        half, fourth, part = size // 2, size // 4, size // (4 * self.m)
        tile = 8 if self.bufs[which]["rc"].dtype == f32 else 16
        span = lambda at, rows: pl.ds(pl.multiple_of(at, tile), rows)
        mine = start + self.core * half
        mine_x = mine + self.xbit * fourth
        return which, start, half, fourth, part, span, mine, mine_x

    def local(self, k):
        which, start, half, fourth, part, span, mine, mine_x = self.geometry(k)
        b = self.bufs[which]
        rows, there = span(mine, half), pl.ds(start // 2, half)
        if isinstance(b["src"], tuple):
            pairs = [(src.at[rows], b["loc"].at[i, there]) for i, src in enumerate(b["src"])]
        else:
            pairs = [(b["src"].at[:, rows], b["loc"].at[:, there])]
        return [pltpu.make_async_copy(x, y, self.out_sem.at[2 * i, k]) for i, (x, y) in enumerate(pairs)]

    def give(self, k):
        which, start, half = self.geometry(k)[:3]
        b = self.bufs[which]
        rows = pl.ds(start, 2 * half)
        return pltpu.make_async_copy(b["out"].at[rows], b["dst"].at[rows], self.out_sem.at[1, k])

    def copies(self, k, step):
        which, start, half, fourth, part, span, mine, mine_x = self.geometry(k)
        b = self.bufs[which]
        m, zed = self.m, self.zed

        def one(src, dst, lane, peer):
            return [
                pltpu.make_async_remote_copy(
                    src, dst, self.send_sem.at[lane, k], self.recv_sem.at[lane, k], device_id=peer,
                    device_id_type=MESH,
                )
            ]

        y_rows = pl.ds(start // 2, half)
        if step == 0:
            away = span(start + (1 - self.core) * half, half)
            if isinstance(b["src"], tuple):
                return [
                    one(src.at[away], b["rc"].at[i, y_rows], 5 * i, self.c_peer)[0]
                    for i, src in enumerate(b["src"])
                ]
            return one(b["src"].at[:, away], b["rc"].at[:, y_rows], 0, self.c_peer)
        if step == 1:
            return one(b["rc"].at[1 - self.s, y_rows], b["ry"].at[y_rows], 1, self.y_peer)
        if step == 2:
            away = span(start // 2 + (1 - self.xbit) * fourth, fourth)
            return one(b["ry"].at[away], b["rx"].at[pl.ds(start // 4, fourth)], 2, self.x_peer)
        if step in (3, 4):
            found = []
            for d in range(1, m):
                if step == 3:
                    there = lax.rem(zed + d, m)
                    src = b["rx"].at[span(start // 4 + there * part, part)]
                    dst = b["rz"].at[d - 1, pl.ds(start // (4 * m), part)]
                else:
                    src = dst = b["out"].at[span(mine_x + zed * part, part)]
                found.append(
                    pltpu.make_async_remote_copy(
                        src, dst, self.zs_sem.at[step - 3, k, d - 1], self.zr_sem.at[step - 3, k, d - 1],
                        device_id=self.z_peer(d), device_id_type=MESH,
                    )
                )
            return found
        rows = span(mine_x, fourth) if step == 5 else span(mine, half)
        return one(b["out"].at[rows], b["out"].at[rows], step - 2, self.x_peer if step == 5 else self.c_peer)

    def add(self, k, step):
        which, start, half, fourth, part, span, mine, mine_x = self.geometry(k)
        b = self.bufs[which]
        kind = b["rc"].dtype
        f = lambda v: v.astype(f32)
        y_rows = pl.ds(start // 2, half)
        x_rows = pl.ds(start // 4, fourth)
        if step == 1:
            if "loc" in b:
                for copy in self.local(k):
                    copy.wait()
                mine_part = b["loc"][:, y_rows]
            else:
                mine_part = b["src"][:, span(mine, half)]
            b["rc"][:, y_rows] = (f(b["rc"][:, y_rows]) + f(mine_part)).astype(kind)
        elif step == 2:
            b["ry"][y_rows] = (f(b["ry"][y_rows]) + f(b["rc"][self.s, y_rows])).astype(kind)
        elif step == 3:
            kept = b["ry"][span(start // 2 + self.xbit * fourth, fourth)]
            b["rx"][x_rows] = (f(b["rx"][x_rows]) + f(kept)).astype(kind)
        elif step == 4:
            result = f(b["rx"][span(start // 4 + self.zed * part, part)])
            for d in range(1, self.m):
                result = result + f(b["rz"][d - 1, pl.ds(start // (4 * self.m), part)])
            b["out"][span(mine_x + self.zed * part, part)] = result.astype(kind)

    def stage(self, k, step):
        if step == 0 and "loc" in self.bufs[self.plan[k][0]]:
            for copy in self.local(k):
                copy.start()
        if step > 0:
            for copy in self.copies(k, step - 1):
                copy.wait_recv()
        self.add(k, step)
        if step < 7:
            for copy in self.copies(k, step):
                copy.start()
        else:
            self.give(k).start()

    def finish(self):
        for k in range(len(self.plan)):
            for step in range(7):
                for copy in self.copies(k, step):
                    copy.wait_send()
            self.give(k).wait()


def back_kernel(
    plan, begin, m, blocks,
    aux_ref, p_ref, ci_ref, conv_ref, raw_ref, run_ref, y_ref, dy_ref, state_ref,
    u_ref, g_ref, zg_ref, dgate_ref, normed_hbm, g_hbm, c_hbm, d_hbm, outg_hbm, gate0_hbm, gate1_hbm,
    ingrad_ref, out_sum, gate_sum, conv_sum, small_sum, gain_sum,
    zx_all, rawg_all, dp_ref, buf, d_hidden, wide, d_left, entered, left, sums,
    normed_all, g_all, c_all, d_all, conv_x, small_x, spread_ref, *rest,
):
    step_at = pl.program_id(0)
    size = u_ref.shape[0]
    half = normed_all.shape[1] // 2
    count = zx_all.shape[0] // size
    names = (("loc", "rc", "ry", "rx", "rz", "out"), ("rc", "ry", "rx", "rz", "out"))
    sources = (
        (outg_hbm, out_sum, names[0]), ((gate0_hbm, gate1_hbm), gate_sum, names[0]),
        (conv_x, conv_sum, names[1]), (small_x, small_sum, names[1]),
    )
    bufs, at = [], 0
    for src, dst, held in sources:
        bufs.append(dict(zip(held, rest[at : at + len(held)]), src=src, dst=dst))
        at += len(held)
    load_sem = rest[-1]
    work = Reduction(plan, m, bufs, rest[at : at + 5])
    gains = (rest[at + 5 : at + 13], rest[at + 13 : at + 17])
    loads = [
        pltpu.make_async_copy(src, dst, load_sem.at[i])
        for i, (src, dst) in enumerate(
            ((normed_hbm, normed_all), (g_hbm, g_all), (c_hbm, c_all), (d_hbm, d_all))
        )
    ]

    conv_chunks = [k for k in range(len(plan)) if plan[k][0] == 2]
    small_chunks = [k for k in range(len(plan)) if plan[k][0] == 3]

    def tick(t):
        for k in range(len(plan)):
            late = t - begin[k]
            if plan[k][0] < 2 and 0 <= late < 9 and late != 2:
                work.stage(k, late - (late > 2))

    def slot(q):
        tick(blocks + q)
        for c, k in enumerate(conv_chunks):
            if 2 <= q + 1 - c < 8:
                work.stage(k, q + 1 - c)
        for k in small_chunks:
            if 0 < q < 8:
                work.stage(k, q)
        gain_hop(q - count)

    def gain_hop(hop):
        (gx, gc, gy, ga, gr, gb, gz, gsum), (sent, got, z_sent, z_got) = gains
        me = work.s

        def send(i, src, dst, peer):
            return pltpu.make_async_remote_copy(
                src, dst, sent.at[i], got.at[i], device_id=peer, device_id_type=MESH
            )

        hops = [
            [send(0, gx, gc, work.c_peer)], [send(1, gy.at[1 - me], gr.at[0], work.y_peer)],
            [send(2, ga, gr.at[1], work.x_peer)],
            [
                pltpu.make_async_remote_copy(
                    gb, gz.at[d - 1], z_sent.at[d - 1], z_got.at[d - 1], device_id=work.z_peer(d),
                    device_id_type=MESH,
                )
                for d in range(1, m)
            ],
        ]
        give = pltpu.make_async_copy(gsum, gain_sum, sent.at[3])
        if 0 < hop < 5:
            for copy in hops[hop - 1]:
                copy.wait_recv()
        if hop == 1:
            gy[...] = gx[...] + gc[...]
        elif hop == 2:
            ga[...] = gy[me] + gr[0]
        elif hop == 3:
            gb[...] = ga[...] + gr[1]
        elif hop == 4:
            result = gb[...]
            for d in range(1, m):
                result = result + gz[d - 1]
            gsum[...] = result
            give.start()
        elif hop == 5:
            for copy in hops[0] + hops[1] + hops[2] + hops[3]:
                copy.wait_send()
            give.wait()
        if 0 <= hop < 4:
            for copy in hops[hop]:
                copy.start()

    @pl.when(step_at == 0)
    def _():
        meet(work.peers())
        fill_spread(spread_ref)
        buf[BLOCK:, :] = jnp.zeros((8, XBC), f32)
        d_hidden[...] = jnp.zeros_like(d_hidden)
        dp_ref[...] = jnp.zeros_like(dp_ref)
        dp_ref[:, 44:50, :] = dgate_ref[:, :6, :]
        gains[0][0][...] = jnp.zeros_like(gains[0][0])

    for t in range(blocks):
        @pl.when(step_at == t)
        def _():
            tick(t)
            if t == 0:
                for load in loads:
                    load.start()

    @pl.when(step_at < blocks)
    def _():
        here = pl.ds(pl.multiple_of((blocks - 1 - step_at) * BLOCK, BLOCK), BLOCK)
        scan_back_step(
            here, aux_ref, p_ref, spread_ref, ci_ref, conv_ref, raw_ref, run_ref, y_ref, dy_ref, state_ref,
            zx_all, rawg_all, dp_ref, buf, d_hidden, wide, d_left, entered, left, sums,
        )

    for j in range(count):
        @pl.when(step_at == blocks + j)
        def _():
            if j == 0:
                for load in loads:
                    load.wait()
                if conv_x.shape[1] > XBC:
                    conv_x[:, XBC:] = jnp.zeros((2, conv_x.shape[1] - XBC, half), bf16)
                normed = normed_all[...]
                step_grad = mm(jnp.transpose(rawg_all[...])[:HEADS], normed)
                if small_x.shape[1] > LANES:
                    small_x[:, LANES:] = jnp.zeros((2, small_x.shape[1] - LANES, LANES), f32)
                for i in range(2):
                    for piece in range(half // LANES):
                        at = i * half + piece * LANES
                        row = 56 + piece * HEADS
                        small_x[i, row : row + HEADS, :] = step_grad[:, at : at + LANES]
                small_x[:, :56, :] = dp_ref[...]
                tick(blocks)
                for k in small_chunks:
                    work.stage(k, 0)
                for c, k in enumerate(conv_chunks):
                    _, start, rows = plan[k]
                    for at in range(start, min(start + rows, XBC), 256):
                        turned = jnp.transpose(zx_all[:, at : at + 256])
                        grad = mm(turned, normed).astype(bf16)
                        for i in range(2):
                            conv_x[i, at : at + 256, :] = grad[:, i * half : (i + 1) * half]
                    work.stage(k, 0)
                    if c > 0:
                        work.stage(conv_chunks[c - 1], 1)
                work.stage(conv_chunks[-1], 1)
            here = pl.ds(j * size, size)
            zg, zc, rg = zg_ref[...], zx_all[here, :], rawg_all[here, :HEADS]
            grad = jnp.concatenate(
                [mm(zg, g_all[i]) + mm(zc, c_all[i]) + mm(rg, d_all[i].astype(bf16)) for i in range(2)], axis=1
            )
            p = p_ref[...].astype(f32)
            u = u_ref[...].astype(f32)
            inv = lax.rsqrt(jnp.mean(u * u, axis=-1, keepdims=True) + eps)
            gain_part = total(grad * u * inv)
            for i in range(2):
                for piece in range(half // LANES):
                    at = i * half + piece * LANES
                    gains[0][0][i, piece : piece + 1, :] += gain_part[:, at : at + LANES]
            lifted = grad * gain_row(p)
            mean_u = jnp.mean(lifted * u, axis=-1, keepdims=True)
            ingrad_ref[...] = (
                g_ref[...].astype(f32) + inv * lifted - u * (inv * inv * inv * mean_u)
            ).astype(bf16)
            if j < count - 1:
                slot(j + 1)
            else:
                for q in range(count, max(count + 6, len(conv_chunks) + 7, 8, max(begin) + 9 - blocks)):
                    slot(q)
                work.finish()


def full(a):
    return pl.BlockSpec(a.shape, lambda i: (0,) * a.ndim, pipeline_mode=pl.Buffered(1))


def compute_params(mib=56):
    return pltpu.CompilerParams(
        dimension_semantics=("arbitrary",), vmem_limit_bytes=mib * 1024 * 1024
    )


def rows_of(size, cols, order):
    return pl.BlockSpec((size, cols), lambda i: (order(i), 0))


shape = jax.ShapeDtypeStruct
fwd = lambda i: i


def acc(rows):
    return pl.BlockSpec((2, rows, LANES), lambda i: (0, 0, 0))


def front(layer_in, seg, w_t, w_out, step_t, pack):
    tokens, width = layer_in.shape
    blocks = tokens // BLOCK
    half = width // 2
    rows = lambda cols: rows_of(BLOCK, cols, fwd)
    far_spec = pl.BlockSpec(memory_space=pl.ANY)
    pieces = ((XBC // 16, 4), (INNER // 8, 2), (w_out.shape[0] // 8, 2))
    n = sum(count for _, count in pieces)
    dma, vm = pltpu.SemaphoreType.DMA, pltpu.VMEM
    return pl.pallas_call(
        functools.partial(front_kernel, pieces, blocks),
        grid=(blocks,),
        in_specs=[rows(width), full(seg)] + [far_spec] * 4,
        out_specs=[
            rows(width), rows(XBC), rows(XBC), rows(LANES), rows(LANES), rows(INNER),
            pl.BlockSpec((1, STATE, INNER), lambda i: (i, 0, 0)), pl.BlockSpec((1, 16, BLOCK), lambda i: (i, 0, 0)),
        ]
        + [far_spec] * 5,
        out_shape=[
            shape((tokens, width), bf16), shape((tokens, XBC), bf16), shape((tokens, XBC), f32),
            shape((tokens, LANES), f32), shape((tokens, LANES), f32), shape((tokens, INNER), f32),
            shape((blocks, STATE, INNER), bf16), shape((blocks, 16, BLOCK), f32),
            shape((2, XBC, half), bf16), shape((2, INNER, half), bf16), shape((2,) + w_out.shape, bf16),
            shape((2,) + step_t.shape, f32), shape((2,) + pack.shape, f32),
        ],
        scratch_shapes=[
            vm((BLOCK + 8, XBC), f32), vm((STATE, INNER), f32), vm((3 * BLOCK + 8, INNER), f32),
            vm((BLOCK, INNER), f32), vm((2 * LANES, INNER), bf16),
            vm((2, XBC, half), bf16), vm((2,) + step_t.shape, f32), vm((2,) + pack.shape, f32),
            vm((INNER, half), bf16), vm(w_out.shape, bf16), vm((blocks, 16, BLOCK), f32),
            dma((10,)), dma((2, 2)), dma((4, n)), dma((4, n)),
        ],
        compiler_params=pltpu.CompilerParams(
            dimension_semantics=("arbitrary",), vmem_limit_bytes=56 * 1024 * 1024, collective_id=0,
            has_side_effects=True,
        ),
        cost_estimate=pl.CostEstimate(
            flops=2 * tokens * width * XBC * 4, bytes_accessed=30_000_000, transcendentals=tokens * 5000
        ),
        name="front",
    )(layer_in, seg, w_t, w_out, step_t, pack)


def gate_both(layer_in, normed, cotangent, y, g_all, o_all, pack):
    tokens, width = layer_in.shape
    size = 256
    rows = lambda cols: rows_of(size, cols, fwd)
    return pl.pallas_call(
        k2_kernel,
        grid=(tokens // size,),
        in_specs=[
            rows(width), rows(width), rows(width), rows(INNER), full(g_all), full(o_all), full(pack),
        ],
        out_specs=[rows(width), rows(INNER), rows(INNER), rows(INNER), acc(8)],
        out_shape=[
            shape((tokens, width), bf16), shape((tokens, INNER), bf16), shape((tokens, INNER), f32),
            shape((tokens, INNER), bf16), shape((2, 8, LANES), f32),
        ],
        scratch_shapes=[pltpu.VMEM((size, INNER), f32)] * 4,
        compiler_params=compute_params(),
        cost_estimate=pl.CostEstimate(
            flops=2 * tokens * width * INNER * 4, bytes_accessed=30_000_000, transcendentals=tokens * 5000
        ),
        name="gate_both",
    )(layer_in, normed, cotangent, y, g_all, o_all, pack)


def backward(
    layer_in, cotangent, aux, pack, ci, conv, raw, running, y, dy, states, zx_gate, d_gate, normed,
    g_all, c_all, d_all, out_grad, gate_grads,
):
    tokens, width = layer_in.shape
    blocks = tokens // BLOCK
    size = 256
    late = tokens // size
    half = width // 2
    m = lax.axis_size("rep") // 4

    def padded(rows, kind):
        unit = (16 if kind == bf16 else 8) * 4 * m
        return -(-rows // unit) * unit

    arrays = (
        (padded(out_grad.shape[1], bf16), width, bf16, 3, True), (padded(INNER, bf16), half, bf16, 3, True),
        (padded(XBC, bf16), half, bf16, late, False), (padded(LANES, f32), LANES, f32, 1, False),
    )
    plan, begin = [], []
    first = (0, 3, blocks, blocks)
    for which, (n, _, kind, pieces, _) in enumerate(arrays):
        units = n // ((16 if kind == bf16 else 8) * 4 * m)
        pieces = min(pieces, units)
        edges = [-(-units * i // pieces) * (n // units) for i in range(pieces + 1)]
        for i in range(pieces):
            plan.append((which, edges[i], edges[i + 1] - edges[i]))
            begin.append(first[which] + i if which < 2 else 0)
    grow = lambda a, n: jnp.pad(a, ((0, 0), (0, n - a.shape[1]), (0, 0)))
    out_grad = grow(out_grad, arrays[0][0])
    gate_grads = [grow(a[None], arrays[1][0])[0] for a in gate_grads]
    scratch = []
    for n, c, kind, _, far in arrays:
        if far:
            scratch.append(pltpu.VMEM((2, n // 2, c), kind))
        scratch += [
            pltpu.VMEM((2, n // 2, c), kind), pltpu.VMEM((n // 2, c), kind), pltpu.VMEM((n // 4, c), kind),
            pltpu.VMEM((max(m - 1, 1), n // (4 * m), c), kind), pltpu.VMEM((n, c), kind),
        ]
    chunks = len(plan)
    dma = pltpu.SemaphoreType.DMA
    back = lambda i: jnp.maximum(blocks - 1 - i, 0)
    row = lambda i: jnp.maximum(i - blocks, 0)
    rows = lambda cols: rows_of(BLOCK, cols, back)
    late_rows = lambda cols: rows_of(size, cols, row)
    far_spec = pl.BlockSpec(memory_space=pl.ANY)
    vm = pltpu.VMEM
    return pl.pallas_call(
        functools.partial(back_kernel, tuple(plan), tuple(begin), m, blocks),
        grid=(blocks + late,),
        in_specs=[
            pl.BlockSpec((1, 16, BLOCK), lambda i: (back(i), 0, 0)), full(pack),
            rows(XBC), rows(XBC), rows(LANES), rows(LANES), rows(INNER), rows(INNER),
            pl.BlockSpec((1, STATE, INNER), lambda i: (back(i), 0, 0)),
            late_rows(width), late_rows(width), late_rows(INNER), full(d_gate),
        ]
        + [far_spec] * 7,
        out_specs=[late_rows(width)] + [far_spec] * 5,
        out_shape=[shape((tokens, width), bf16)] + [shape((n, c), kind) for n, c, kind, _, _ in arrays]
        + [shape((8, LANES), f32)],
        scratch_shapes=[
            vm((tokens, XBC), bf16), vm((tokens, LANES), bf16), vm((2, 56, LANES), f32),
            vm((BLOCK + 8, XBC), f32), vm((STATE, INNER), f32), vm((3 * BLOCK + 8, INNER), f32),
            vm((BLOCK, INNER), f32), vm((BLOCK, INNER), bf16), vm((BLOCK, INNER), bf16),
            vm((4 * BLOCK + 32, INNER), bf16),
            vm(normed.shape, bf16), vm(g_all.shape, bf16), vm(c_all.shape, bf16), vm(d_all.shape, f32),
            vm((2, arrays[2][0], half), bf16), vm((2, arrays[3][0], LANES), f32),
            vm((2 * LANES, INNER), bf16),
        ]
        + scratch
        + [
            dma((6, chunks)), dma((6, chunks)), dma((2, chunks, max(m - 1, 1))),
            dma((2, chunks, max(m - 1, 1))), dma((3, chunks)),
            vm((2, 8, LANES), f32), vm((2, 8, LANES), f32), vm((2, 8, LANES), f32), vm((8, LANES), f32),
            vm((2, 8, LANES), f32), vm((8, LANES), f32), vm((max(m - 1, 1), 8, LANES), f32), vm((8, LANES), f32),
            dma((4,)), dma((3,)), dma((max(m - 1, 1),)), dma((max(m - 1, 1),)), dma((4,)),
        ],
        compiler_params=pltpu.CompilerParams(
            dimension_semantics=("arbitrary",), vmem_limit_bytes=62 * 1024 * 1024, collective_id=1,
            has_side_effects=True,
        ),
        cost_estimate=pl.CostEstimate(
            flops=2 * tokens * 768 * XBC * 8, bytes_accessed=40_000_000, transcendentals=tokens * 5000
        ),
        name="backward_reduce",
    )(aux, pack, ci, conv, raw, running, y, dy, states, layer_in, cotangent, zx_gate, d_gate,
      normed, g_all, c_all, d_all, out_grad, *gate_grads)


def pack_rows(norm_gain, conv_weight, conv_bias, dt_bias, a_log, skip_gain, gate_gain):
    pieces = (norm_gain, conv_weight.reshape(-1), conv_bias, gate_gain, dt_bias, a_log, skip_gain)
    size, at, flat = 48 * LANES, 0, None
    for v in pieces:
        wide = jnp.pad(v.astype(f32), (at, size - at - v.size))
        flat = wide if flat is None else flat + wide
        at += -(-v.size // LANES) * LANES
    return flat.reshape(-1, LANES)


def body(
    layer_in, segment_ids, cotangent, norm_gain, in_weight, conv_weight, conv_bias, dt_bias, a_log,
    skip_gain, gate_gain, out_weight,
):
    width = layer_in.shape[1]
    w_t = in_weight.T
    pack = pack_rows(norm_gain, conv_weight, conv_bias, dt_bias, a_log, skip_gain, gate_gain)
    step_t = w_t[WIDE:].astype(f32)
    normed, ci, conv, raw, running, y, states, aux, c_all, g_all, o_all, d_all, p_all = front(
        layer_in, segment_ids.reshape(-1, LANES), w_t, out_weight, step_t, pack
    )
    layer_out, mixed, dy, zx_gate, d_gate = gate_both(layer_in, normed, cotangent, y, g_all, o_all, p_all)
    nt = ((0,), (0,))
    half = width // 2
    by_half = lambda a: [mm(a, normed[:, i * half : (i + 1) * half], nt).astype(bf16) for i in range(2)]
    out_grad = mm(mixed, cotangent, nt).astype(bf16).reshape(2, -1, width)
    gate_grads = by_half(zx_gate)
    input_grad, out_sum, gate_sum, conv_sum, small_sum, gain_sum = backward(
        layer_in, cotangent, aux, p_all, ci, conv, raw, running, y, dy, states, zx_gate, d_gate,
        normed, g_all, c_all, d_all, out_grad, gate_grads,
    )
    factor = 1.0 / (lax.axis_size("shard") * lax.axis_size("rep"))
    small_sum = small_sum * factor
    pieces = half // LANES
    step_sum = small_sum[56 : 56 + pieces * HEADS].reshape(pieces, HEADS, LANES).transpose(1, 0, 2).reshape(HEADS, half)
    in_weight_grad = jnp.concatenate(
        [gate_sum[:INNER].astype(f32) * factor, conv_sum[:XBC].astype(f32) * factor, step_sum], axis=0
    ).T
    own = dt_bias.size
    head = lambda k: lax.dynamic_slice(small_sum[50 + k], (lax.axis_index("shard") * own,), (own,))
    return (
        layer_out, input_grad, (gain_sum[:3] * factor).reshape(norm_gain.shape), in_weight_grad,
        small_sum[3:31].reshape(conv_weight.shape), small_sum[31:38].reshape(conv_bias.shape),
        head(0), head(1), small_sum[38:44].reshape(own, HEADDIM).sum(axis=1),
        small_sum[44:50].reshape(gate_gain.shape), out_sum[: out_weight.shape[0]].astype(f32) * factor,
    )


def solution(mesh):
    both, shard = P(("shard", "rep"), None), P("shard")
    in_specs = (
        both, both, both, shard, P("shard", None), P(None, "shard"), shard, shard, shard, shard, shard,
        P("shard", None),
    )
    out_specs = (
        both, both, shard, P("shard", None), P(None, "shard"), shard, shard, shard, shard, shard,
        P("shard", None),
    )
    return jax.shard_map(body, mesh=mesh, in_specs=in_specs, out_specs=out_specs, check_vma=False)
```

```python
import functools

import jax
import jax.numpy as jnp
from jax import lax
from jax.experimental import pallas as pl
from jax.experimental.pallas import tpu as pltpu
from jax.sharding import PartitionSpec as P

HEADS = 24
HEADDIM = 64
STATE = 128
CONV = 4
BLOCK = 128
INNER = 1536
XBC = 1792
WIDE = INNER + XBC
LANES = 128
LOG2E = 1.4426950408889634

MESH = pl.DeviceIdType.MESH
eps = 1e-05
highest = lax.Precision.HIGHEST
f32 = jnp.float32
bf16 = jnp.bfloat16


def mm(a, b, contract=((1,), (0,))):
    return lax.dot_general(a, b, (contract, ((), ())), preferred_element_type=f32)


def mm_t(a, w_ref):
    half = w_ref.shape[2]
    nt = ((1,), (1,))
    return mm(a[:, :half], w_ref[0], nt) + mm(a[:, half:], w_ref[1], nt)


def total(v):
    return jnp.sum(v, axis=0, keepdims=True)


def sigmoid(v):
    return 0.5 + 0.5 * jnp.tanh(0.5 * v)


def softplus(v):
    small = jnp.exp(-jnp.abs(v))
    series = small * (1.0 - small * (0.5 - small * (1.0 / 3.0 - small * 0.25)))
    return jnp.maximum(v, 0.0) + jnp.where(small < 0.03, series, jnp.log(1.0 + small))


def spread(per_head, spread_mat):
    high = per_head.astype(bf16)
    rest = (per_head - high.astype(f32)).astype(bf16)
    return mm(jnp.concatenate([high, rest], axis=1), spread_mat)


def gain_row(p):
    return jnp.concatenate([p[i, j : j + 1, :] for i in range(2) for j in range(3)], axis=1)


def conv_tap(p, tap, j):
    at = 3 + tap * 7 + j % 7
    return p[j // 7, at : at + 1, :]


def conv_bias(p, j):
    return p[j // 7, 31 + j % 7 : 32 + j % 7, :]


def gate_row(p, pair):
    return p[pair // 6, 38 + pair % 6 : 39 + pair % 6, :]


def head_rows(p):
    return p[0, 40:48, :] + pltpu.roll(p[1, 40:48, :], HEADS // 2, 1)


def fill_spread(ref):
    row = lax.broadcasted_iota(jnp.int32, ref.shape, 0) & (LANES - 1)
    col = lax.broadcasted_iota(jnp.int32, ref.shape, 1)
    ref[...] = jnp.where(row == lax.shift_right_logical(col, 6), 1.0, 0.0).astype(bf16)


def lane_pair(values, first):
    lane = lax.broadcasted_iota(jnp.int32, values.shape, 1)
    zero = jnp.zeros_like(values)
    return jnp.concatenate(
        [jnp.where(lane < HEADDIM, values, zero), jnp.where(lane >= HEADDIM, values, zero)], axis=0
    )


def spread_of(running, running_t, head):
    diff = running[:, head : head + 1] - running_t[head : head + 1, :]
    return jnp.exp2(jnp.minimum(diff, 0.0))


def spread_back(running, running_t, head):
    diff = running_t[head : head + 1, :] - running[:, head : head + 1]
    return jnp.exp2(jnp.minimum(diff, 0.0))


def exchange_ids():
    s, r = lax.axis_index("shard"), lax.axis_index("rep")
    flip = lambda b: r + b - 2 * b * (lax.rem(lax.div(r, b), 2))
    return s, r, flip


def meet(peers):
    barrier = pltpu.get_barrier_semaphore()
    for peer in peers:
        pl.semaphore_signal(barrier, inc=1, device_id=peer, device_id_type=MESH)
    pl.semaphore_wait(barrier, len(peers))


def scan_forward_step(
    u_ref, aux_ref, c_ref, d_ref, p_ref, spread_ref, normed_ref, ci_ref, conv_ref, raw_ref, run_ref, y_ref,
    state_ref, buf, hidden, wide, inter,
):
    p = p_ref[...].astype(f32)
    heads_at = head_rows(p)
    u = u_ref[...].astype(f32)
    inv = lax.rsqrt(jnp.mean(u * u, axis=-1, keepdims=True) + eps)
    normed = (u * inv * gain_row(p)).astype(bf16)
    normed_ref[...] = normed
    buf[8 : 8 + BLOCK, :] = mm_t(normed, c_ref)
    half = normed.shape[1] // 2
    raw = sum(mm(normed[:, i * half : (i + 1) * half], d_ref[i].astype(bf16), ((1,), (1,))) for i in range(2))
    raw_ref[:, : raw.shape[1]] = raw
    raw_ref[:, raw.shape[1] :] = jnp.zeros((BLOCK, LANES - raw.shape[1]), f32)
    aux = jnp.transpose(aux_ref[0])
    masks = [jnp.broadcast_to(aux[:, k : k + 1], (BLOCK, LANES)) for k in range(3)]
    step = softplus(raw_ref[...] + heads_at[4:5, :])
    decay = (-LOG2E) * jnp.exp(heads_at[5:6, :]) * step
    row = lax.broadcasted_iota(jnp.int32, (BLOCK, BLOCK), 0)
    col = lax.broadcasted_iota(jnp.int32, (BLOCK, BLOCK), 1)
    lower = (row >= col).astype(f32)
    running = lax.dot_general(
        lower, decay, (((1,), (0,)), ((), ())), precision=highest, preferred_element_type=f32
    )
    run_ref[...] = running
    running_t = jnp.transpose(running)
    entering = jnp.exp2(running) * aux[:, 3:4]
    leaving = jnp.exp2(running[BLOCK - 1 : BLOCK, :] - running) * aux[:, 4:5]
    wide[...] = spread(jnp.concatenate([step, entering, leaving, heads_at], axis=0), spread_ref[...])

    def conv_chunk(j):
        cols = slice(j * LANES, (j + 1) * LANES)
        x = buf[8 : 8 + BLOCK, cols]
        ci_ref[:, cols] = x.astype(bf16)
        conv = conv_bias(p, j) + conv_tap(p, CONV - 1, j) * x
        for k in range(1, CONV):
            conv = conv + conv_tap(p, CONV - 1 - k, j) * (buf[8 - k : 8 - k + BLOCK, cols] * masks[k - 1])
        conv_ref[:, cols] = conv
        return conv * sigmoid(conv)

    b_low = conv_chunk(HEADS // 2).astype(bf16)
    c_low = conv_chunk(HEADS // 2 + 1).astype(bf16)
    b_t = jnp.transpose(b_low)
    allowed = (row >= col) & (aux[:, 5:6] == aux_ref[0, 5:6, :])
    scores = jnp.where(allowed, mm(c_low, b_low, ((1,), (1,))), 0.0)
    state_low = hidden[...].astype(bf16)
    state_ref[0] = state_low
    inter[...] = mm(c_low, state_low)
    for pair in range(HEADS // 2):
        cols = slice(pair * LANES, (pair + 1) * LANES)
        values = conv_chunk(pair)
        weighted = values * wide[0:BLOCK, cols]
        first = (spread_of(running, running_t, 2 * pair) * scores).astype(bf16)
        second = (spread_of(running, running_t, 2 * pair + 1) * scores).astype(bf16)
        enter = wide[BLOCK : 2 * BLOCK, cols]
        y_ref[:, cols] = (
            mm(jnp.concatenate([first, second], axis=1), lane_pair(weighted.astype(bf16), pair))
            + inter[:, cols] * enter
            + wide[3 * BLOCK + 6 : 3 * BLOCK + 7, cols] * values
        )
        left = (weighted * wide[2 * BLOCK : 3 * BLOCK, cols]).astype(bf16)
        hidden[:, cols] = hidden[:, cols] * wide[2 * BLOCK - 1 : 2 * BLOCK, cols] + mm(b_t, left)
    buf[0:8, :] = buf[BLOCK : BLOCK + 8, :]


def segment_masks(seg, aux_all):
    blocks = seg.shape[0]
    block = lax.broadcasted_iota(jnp.int32, seg.shape, 0)
    lane = lax.broadcasted_iota(jnp.int32, seg.shape, 1)
    last = jnp.sum(jnp.where(lane == LANES - 1, seg, 0.0), axis=1, keepdims=True)
    last = jnp.broadcast_to(last, seg.shape)
    before = jnp.where(block == 0, -1.0, pltpu.roll(seg, 1, 0))
    after = jnp.where(block == blocks - 1, -1.0, pltpu.roll(seg, blocks - 1, 0))
    rows = []
    for k in range(1, CONV):
        other = jnp.where(lane >= k, pltpu.roll(seg, k, 1), pltpu.roll(before, k, 1))
        rows.append(other == seg)
    rows.append(jnp.where(block == 0, -1.0, pltpu.roll(last, 1, 0)) == seg)
    rows.append(last == seg)
    rows.append(seg)
    for k in range(1, CONV):
        other = jnp.where(lane < LANES - k, pltpu.roll(seg, LANES - k, 1), pltpu.roll(after, LANES - k, 1))
        rows.append(other == seg)
    aux_all[...] = jnp.zeros_like(aux_all)
    for at, value in enumerate(rows):
        value = value if value.dtype == f32 else jnp.where(value, 1.0, 0.0)
        for b in range(blocks):
            aux_all[b, at : at + 1, :] = value[b : b + 1, :]


class Gather:
    def __init__(self, pieces, sections, send_sem, recv_sem):
        s, r, flip = exchange_ids()
        self.s, self.pieces, self.sections = s, pieces, sections
        self.send_sem, self.recv_sem = send_sem, recv_sem
        self.y_peer, self.x_peer, self.c_peer = (1 - s, r), (s, flip(2)), (s, flip(1))
        self.quarter, self.x_quarter = lax.rem(r, 4), lax.rem(flip(2), 4)
        self.todo = [(which, piece) for which, (_, count) in enumerate(pieces) for piece in range(count)]

    def rows_at(self, which, part, piece, base=0):
        size, count = self.pieces[which]
        return pl.ds(pl.multiple_of(base + (part * count + piece) * size, 16), size)

    def copy(self, k, lane):
        which, piece = self.todo[k]
        src, base, dst = self.sections[which]
        if lane == 0:
            block = src.at[self.rows_at(which, self.quarter, piece, base)]
            there = dst.at[self.s, self.rows_at(which, self.quarter, piece)]
        else:
            part = self.x_quarter if lane == 3 else self.quarter
            block = there = dst.at[1 - self.s, self.rows_at(which, part, piece)]
        return pltpu.make_async_remote_copy(
            block, there, self.send_sem.at[lane, k], self.recv_sem.at[lane, k],
            device_id=(self.y_peer, self.x_peer, self.c_peer, self.c_peer)[lane], device_id_type=MESH,
        )

    def near(self, k):
        self.copy(k, 0).wait_recv()
        self.copy(k, 1).start()
        self.copy(k, 2).start()

    def far(self, k):
        self.copy(k, 1).wait_recv()
        self.copy(k, 3).start()

    def finish(self, ks):
        for k in ks:
            for lane in (2, 3):
                self.copy(k, lane).wait_recv()

    def sent(self):
        for k in range(len(self.todo)):
            for lane in range(4):
                self.copy(k, lane).wait_send()


def front_kernel(
    pieces, blocks,
    u_ref, seg_ref, w_hbm, o_hbm, d_hbm, p_hbm,
    normed_ref, ci_ref, conv_ref, raw_ref, run_ref, y_ref, state_ref, aux_out, c_out, g_all, o_all, d_out, p_out,
    buf, hidden, wide, inter, spread_ref, c_all, d_all, p_all, g_stage, o_stage, aux_all,
    local_sem, small_sem, send_sem, recv_sem,
):
    step_at = pl.program_id(0)
    sections = ((w_hbm, INNER, c_all), (w_hbm, 0, g_all), (o_hbm, 0, o_all))
    work = Gather(pieces, sections, send_sem, recv_sem)
    s = work.s
    urgent = range(pieces[0][1])
    later = range(pieces[0][1], len(work.todo))
    small = [
        pltpu.make_async_remote_copy(
            src, dst.at[s], small_sem.at[0, i], small_sem.at[1, i], device_id=work.y_peer, device_id_type=MESH
        )
        for i, (src, dst) in enumerate(((d_hbm, d_all), (p_hbm, p_all)))
    ]
    own = [
        pltpu.make_async_copy(src, dst, local_sem.at[i])
        for i, (src, dst) in enumerate(
            (
                (d_hbm, d_all.at[s]), (p_hbm, p_all.at[s]), (w_hbm.at[pl.ds(INNER, XBC)], c_all.at[s]),
                (w_hbm.at[pl.ds(0, INNER)], g_stage), (o_hbm, o_stage),
            )
        )
    ]
    back = [
        pltpu.make_async_copy(src, dst, local_sem.at[5 + i])
        for i, (src, dst) in enumerate(
            ((d_all, d_out), (p_all, p_out), (c_all, c_out), (g_stage, g_all.at[s]), (o_stage, o_all.at[s]))
        )
    ]

    @pl.when(step_at == 0)
    def _():
        meet((work.y_peer, work.x_peer, work.c_peer))
        for copy in small:
            copy.start()
        for k in urgent:
            work.copy(k, 0).start()
        for copy in own:
            copy.start()
        buf[0:8, :] = jnp.zeros((8, XBC), f32)
        hidden[...] = jnp.zeros_like(hidden)
        fill_spread(spread_ref)
        for k in urgent:
            work.near(k)
            if k > 0:
                work.far(k - 1)
        for k in later[:2]:
            work.copy(k, 0).start()
        work.far(urgent[-1])
        for copy in small + own[:3]:
            copy.wait()
        work.finish(urgent)
        segment_masks(seg_ref[...].astype(f32), aux_all)

    for t in range(1, blocks):
        @pl.when(step_at == t)
        def _():
            if t == 1:
                for copy in own[3:]:
                    copy.wait()
                for copy in back:
                    copy.start()
            for i, k in enumerate(later):
                if t == i - 1:
                    work.copy(k, 0).start()
                if t == 2 + i:
                    work.near(k)
                if t == 4 + i:
                    work.far(k)

    aux_out[0] = aux_all[step_at]
    scan_forward_step(
        u_ref, aux_all.at[pl.ds(step_at, 1)], c_all, d_all, p_all, spread_ref, normed_ref, ci_ref, conv_ref, raw_ref, run_ref, y_ref,
        state_ref, buf, hidden, wide, inter,
    )

    @pl.when(step_at == blocks - 1)
    def _():
        for i, k in enumerate(later):
            if i - 1 >= blocks:
                work.copy(k, 0).start()
            if 2 + i >= blocks:
                work.near(k)
        for i, k in enumerate(later):
            if 4 + i >= blocks:
                work.far(k)
        work.finish(later)
        work.sent()
        for copy in back:
            copy.wait()


def k2_kernel(
    u_ref, normed_ref, g_ref, y_ref, g_all_ref, o_ref, p_ref,
    out_ref, mixed_ref, dy_ref, zx_ref, dgate_ref,
    gate, mixed_grad, gated, sig,
):
    rows = u_ref.shape[0]

    @pl.when(pl.program_id(0) == 0)
    def _():
        dgate_ref[...] = jnp.zeros_like(dgate_ref)

    p = p_ref[...].astype(f32)
    gate[...] = mm_t(normed_ref[...], g_all_ref)
    out_w = o_ref[...].reshape(INNER, -1)
    mixed_grad[...] = mm(g_ref[...], out_w, ((1,), (1,)))
    SUB = 64
    for sub in range(rows // SUB):
        r = slice(sub * SUB, (sub + 1) * SUB)
        square = jnp.zeros((SUB, LANES), f32)
        cross = jnp.zeros((SUB, LANES), f32)
        for pair in range(HEADS // 2):
            cols = slice(pair * LANES, (pair + 1) * LANES)
            v = gate[r, cols]
            s = sigmoid(v)
            sig[r, cols] = s
            product = y_ref[r, cols] * (v * s)
            gated[r, cols] = product
            square = square + product * product
            cross = cross + mixed_grad[r, cols] * gate_row(p, pair) * product
        inv = lax.rsqrt(jnp.sum(square, axis=-1, keepdims=True) * (1.0 / INNER) + eps)
        back = inv * inv * inv * (jnp.sum(cross, axis=-1, keepdims=True) * (1.0 / INNER))
        inv = jnp.broadcast_to(inv, (SUB, LANES))
        back = jnp.broadcast_to(back, (SUB, LANES))
        for pair in range(HEADS // 2):
            cols = slice(pair * LANES, (pair + 1) * LANES)
            v, s, product = gate[r, cols], sig[r, cols], gated[r, cols]
            scaled = product * inv
            gain = gate_row(p, pair)
            mixed_ref[r, cols] = (scaled * gain).astype(bf16)
            mg = mixed_grad[r, cols]
            dgate_ref[pair // 6, pair % 6 : pair % 6 + 1, :] += total(mg * scaled)
            d_gated = inv * (mg * gain) - product * back
            act = v * s
            dy_ref[r, cols] = d_gated * act
            zx_ref[r, cols] = (d_gated * y_ref[r, cols] * (s + act * (1.0 - s))).astype(bf16)
    out_ref[...] = (u_ref[...].astype(f32) + mm(mixed_ref[...], out_w)).astype(bf16)


def scan_back_step(
    here, aux_ref, p_ref, spread_ref, ci_ref, conv_ref, raw_ref, run_ref, y_ref, dy_ref, state_ref,
    zx_all, rawg_all, dp_ref, buf, d_hidden, wide, d_left, entered, left, sums,
):
    p = p_ref[...].astype(f32)
    heads_at = head_rows(p)
    aux = jnp.transpose(aux_ref[0])
    masks = [jnp.broadcast_to(aux[:, k : k + 1], (BLOCK, LANES)) for k in range(6, 9)]
    pre = raw_ref[...] + heads_at[4:5, :]
    step = softplus(pre)
    rate = -jnp.exp(heads_at[5:6, :])
    running = run_ref[...]
    running_t = jnp.transpose(running)
    entering = jnp.exp2(running) * aux[:, 3:4]
    leaving = jnp.exp2(running[BLOCK - 1 : BLOCK, :] - running) * aux[:, 4:5]
    spread_mat = spread_ref[...]
    wide[...] = spread(jnp.concatenate([step, entering, leaving, heads_at], axis=0), spread_mat)

    def act_chunk(j):
        cols = slice(j * LANES, (j + 1) * LANES)
        conv = conv_ref[:, cols]
        sig = sigmoid(conv)
        act = conv * sig
        return act, sig + act * (1.0 - sig)

    def conv_back(j, d_conv):
        cols = slice(j * LANES, (j + 1) * LANES)
        buf[:BLOCK, cols] = d_conv
        ci = ci_ref[:, cols].astype(f32)
        shard, at = j // 7, j % 7
        dp_ref[shard, 31 + at : 32 + at, :] += total(d_conv)
        dp_ref[shard, 24 + at : 25 + at, :] += total(ci * d_conv)
        d_in = conv_tap(p, CONV - 1, j) * d_conv
        for k in range(1, CONV):
            later = buf[k : BLOCK + k, cols] * masks[k - 1]
            d_in = d_in + conv_tap(p, CONV - 1 - k, j) * later
            row_at = 3 + (CONV - 1 - k) * 7 + at
            dp_ref[shard, row_at : row_at + 1, :] += total(ci * later)
        zx_all[here, cols] = d_in.astype(bf16)
        buf[BLOCK:, cols] = d_conv[:8, :]

    b_act, b_slope = act_chunk(HEADS // 2)
    c_act, c_slope = act_chunk(HEADS // 2 + 1)
    b_low, c_low = b_act.astype(bf16), c_act.astype(bf16)
    c_t = jnp.transpose(c_low)
    row = lax.broadcasted_iota(jnp.int32, (BLOCK, BLOCK), 0)
    col = lax.broadcasted_iota(jnp.int32, (BLOCK, BLOCK), 1)
    allowed_t = (col >= row) & (aux[:, 5:6] == aux_ref[0, 5:6, :])
    scores_t = jnp.where(allowed_t, mm(b_low, c_low, ((1,), (1,))), 0.0)
    d_state_low = d_hidden[...].astype(bf16)
    d_left[...] = mm(b_low, d_state_low)
    d_scores_t = jnp.zeros((BLOCK, BLOCK), f32)
    for pair in range(HEADS // 2):
        cols = slice(pair * LANES, (pair + 1) * LANES)
        values, slope = act_chunk(pair)
        step_wide = wide[0:BLOCK, cols]
        enter = wide[BLOCK : 2 * BLOCK, cols]
        leave = wide[2 * BLOCK : 3 * BLOCK, cols]
        dy = dy_ref[:, cols]
        skip = wide[3 * BLOCK + 6 : 3 * BLOCK + 7, cols]
        weighted = values * step_wide
        left[:, cols] = (weighted * leave).astype(bf16)
        entered_low = (dy * enter).astype(bf16)
        entered[:, cols] = entered_low
        dp_ref[pair // 6, 38 + pair % 6 : 39 + pair % 6, :] += total(dy * values)
        dy_low = dy.astype(bf16)
        w_low = weighted.astype(bf16)
        d_kernel = mm(lane_pair(w_low, pair), dy_low, ((1,), (1,)))
        spread_a = spread_back(running, running_t, 2 * pair)
        spread_b = spread_back(running, running_t, 2 * pair + 1)
        d_scores_t = d_scores_t + (d_kernel[:BLOCK] * spread_a + d_kernel[BLOCK:] * spread_b)
        kernel_two = jnp.concatenate(
            [(spread_a * scores_t).astype(bf16), (spread_b * scores_t).astype(bf16)], axis=1
        )
        d_leave = d_left[:, cols] * leave
        d_weighted = mm(kernel_two, lane_pair(dy_low, pair)) + d_leave
        w_kept = w_low.astype(f32)
        flow_in = dy_low.astype(f32) * (y_ref[:, cols] - skip * values) - w_kept * d_weighted
        flow_out = d_weighted * values
        for k, flow in enumerate((flow_in, flow_out)):
            high = flow.astype(bf16)
            sums[2 * k * BLOCK : (2 * k + 1) * BLOCK, cols] = high
            sums[(2 * k + 1) * BLOCK : (2 * k + 2) * BLOCK, cols] = (flow - high.astype(f32)).astype(bf16)
        carried = wide[2 * BLOCK - 1 : 2 * BLOCK, cols]
        d_state = d_hidden[:, cols]
        end = total(w_kept * d_leave) + total(d_state * state_ref[0, :, cols].astype(f32)) * carried
        high = end.astype(bf16)
        sums[4 * BLOCK : 4 * BLOCK + 16, cols] = jnp.broadcast_to(high, (16, LANES))
        sums[4 * BLOCK + 16 :, cols] = jnp.broadcast_to((end - high.astype(f32)).astype(bf16), (16, LANES))
        d_hidden[:, cols] = d_state * carried + mm(c_t, entered_low)
        conv_back(pair, (dy * skip + d_weighted * step_wide) * slope)
    d_scores_low = jnp.where(allowed_t, d_scores_t, 0.0).astype(bf16)
    state_low = state_ref[0]
    d_b = mm(left[...], d_state_low, ((1,), (1,))) + mm(d_scores_low, c_low)
    d_c = mm(entered[...], state_low, ((1,), (1,))) + mm(d_scores_low, b_low, ((0,), (0,)))
    conv_back(HEADS // 2, d_b * b_slope)
    conv_back(HEADS // 2 + 1, d_c * c_slope)
    heads = mm(sums[...], spread_mat[:LANES, :], ((1,), (1,)))
    d_step = heads[2 * BLOCK : 3 * BLOCK] + heads[3 * BLOCK : 4 * BLOCK]
    d_running = heads[:BLOCK] + heads[BLOCK : 2 * BLOCK]
    d_end = heads[4 * BLOCK : 4 * BLOCK + 1] + heads[4 * BLOCK + 16 : 4 * BLOCK + 17]
    upper = (col >= row).astype(f32)
    d_decay = d_end + lax.dot_general(
        upper, d_running, (((1,), (0,)), ((), ())), precision=highest, preferred_element_type=f32
    )
    d_raw = (d_step + d_decay * rate) * sigmoid(pre)
    raw_sum, log_sum = total(d_raw), total(d_decay * rate * step)
    for shard in range(2):
        dp_ref[shard, 50:51, :] += raw_sum
        dp_ref[shard, 51:52, :] += log_sum
    rawg_all[here, :] = d_raw.astype(bf16)


class Reduction:
    def __init__(self, plan, m, bufs, sems):
        self.plan, self.m, self.bufs = plan, m, bufs
        self.send_sem, self.recv_sem, self.zs_sem, self.zr_sem, self.out_sem = sems
        s, r, flip = exchange_ids()
        self.s, self.r = s, r
        self.core, self.xbit, self.zed = lax.rem(r, 2), lax.rem(lax.div(r, 2), 2), lax.div(r, 4)
        self.y_peer, self.x_peer, self.c_peer = (1 - s, r), (s, flip(2)), (s, flip(1))

    def z_peer(self, d):
        return (self.s, lax.rem(self.zed + d, self.m) * 4 + lax.rem(self.r, 4))

    def peers(self):
        return (self.y_peer, self.x_peer, self.c_peer) + tuple(self.z_peer(d) for d in range(1, self.m))

    def geometry(self, k):
        which, start, size = self.plan[k]
        half, fourth, part = size // 2, size // 4, size // (4 * self.m)
        tile = 8 if self.bufs[which]["rc"].dtype == f32 else 16
        span = lambda at, rows: pl.ds(pl.multiple_of(at, tile), rows)
        mine = start + self.core * half
        mine_x = mine + self.xbit * fourth
        return which, start, half, fourth, part, span, mine, mine_x

    def local(self, k):
        which, start, half, fourth, part, span, mine, mine_x = self.geometry(k)
        b = self.bufs[which]
        rows, there = span(mine, half), pl.ds(start // 2, half)
        if isinstance(b["src"], tuple):
            pairs = [(src.at[rows], b["loc"].at[i, there]) for i, src in enumerate(b["src"])]
        else:
            pairs = [(b["src"].at[:, rows], b["loc"].at[:, there])]
        return [pltpu.make_async_copy(x, y, self.out_sem.at[2 * i, k]) for i, (x, y) in enumerate(pairs)]

    def give(self, k):
        which, start, half = self.geometry(k)[:3]
        b = self.bufs[which]
        rows = pl.ds(start, 2 * half)
        return pltpu.make_async_copy(b["out"].at[rows], b["dst"].at[rows], self.out_sem.at[1, k])

    def copies(self, k, step):
        which, start, half, fourth, part, span, mine, mine_x = self.geometry(k)
        b = self.bufs[which]
        m, zed = self.m, self.zed

        def one(src, dst, lane, peer):
            return [
                pltpu.make_async_remote_copy(
                    src, dst, self.send_sem.at[lane, k], self.recv_sem.at[lane, k], device_id=peer,
                    device_id_type=MESH,
                )
            ]

        y_rows = pl.ds(start // 2, half)
        if step == 0:
            away = span(start + (1 - self.core) * half, half)
            if isinstance(b["src"], tuple):
                return [
                    one(src.at[away], b["rc"].at[i, y_rows], 5 * i, self.c_peer)[0]
                    for i, src in enumerate(b["src"])
                ]
            return one(b["src"].at[:, away], b["rc"].at[:, y_rows], 0, self.c_peer)
        if step == 1:
            return one(b["rc"].at[1 - self.s, y_rows], b["ry"].at[y_rows], 1, self.y_peer)
        if step == 2:
            away = span(start // 2 + (1 - self.xbit) * fourth, fourth)
            return one(b["ry"].at[away], b["rx"].at[pl.ds(start // 4, fourth)], 2, self.x_peer)
        if step in (3, 4):
            found = []
            for d in range(1, m):
                if step == 3:
                    there = lax.rem(zed + d, m)
                    src = b["rx"].at[span(start // 4 + there * part, part)]
                    dst = b["rz"].at[d - 1, pl.ds(start // (4 * m), part)]
                else:
                    src = dst = b["out"].at[span(mine_x + zed * part, part)]
                found.append(
                    pltpu.make_async_remote_copy(
                        src, dst, self.zs_sem.at[step - 3, k, d - 1], self.zr_sem.at[step - 3, k, d - 1],
                        device_id=self.z_peer(d), device_id_type=MESH,
                    )
                )
            return found
        rows = span(mine_x, fourth) if step == 5 else span(mine, half)
        return one(b["out"].at[rows], b["out"].at[rows], step - 2, self.x_peer if step == 5 else self.c_peer)

    def add(self, k, step):
        which, start, half, fourth, part, span, mine, mine_x = self.geometry(k)
        b = self.bufs[which]
        kind = b["rc"].dtype
        f = lambda v: v.astype(f32)
        y_rows = pl.ds(start // 2, half)
        x_rows = pl.ds(start // 4, fourth)
        if step == 1:
            if "loc" in b:
                for copy in self.local(k):
                    copy.wait()
                mine_part = b["loc"][:, y_rows]
            else:
                mine_part = b["src"][:, span(mine, half)]
            b["rc"][:, y_rows] = (f(b["rc"][:, y_rows]) + f(mine_part)).astype(kind)
        elif step == 2:
            b["ry"][y_rows] = (f(b["ry"][y_rows]) + f(b["rc"][self.s, y_rows])).astype(kind)
        elif step == 3:
            kept = b["ry"][span(start // 2 + self.xbit * fourth, fourth)]
            b["rx"][x_rows] = (f(b["rx"][x_rows]) + f(kept)).astype(kind)
        elif step == 4:
            result = f(b["rx"][span(start // 4 + self.zed * part, part)])
            for d in range(1, self.m):
                result = result + f(b["rz"][d - 1, pl.ds(start // (4 * self.m), part)])
            b["out"][span(mine_x + self.zed * part, part)] = result.astype(kind)

    def stage(self, k, step):
        if step == 0 and "loc" in self.bufs[self.plan[k][0]]:
            for copy in self.local(k):
                copy.start()
        if step > 0:
            for copy in self.copies(k, step - 1):
                copy.wait_recv()
        self.add(k, step)
        if step < 7:
            for copy in self.copies(k, step):
                copy.start()
        else:
            self.give(k).start()

    def finish(self):
        for k in range(len(self.plan)):
            for step in range(7):
                for copy in self.copies(k, step):
                    copy.wait_send()
            self.give(k).wait()


def back_kernel(
    plan, begin, m, blocks,
    aux_ref, p_ref, ci_ref, conv_ref, raw_ref, run_ref, y_ref, dy_ref, state_ref,
    u_ref, g_ref, zg_ref, dgate_ref, normed_hbm, g_hbm, c_hbm, d_hbm, outg_hbm, gate0_hbm, gate1_hbm,
    ingrad_ref, out_sum, gate_sum, conv_sum, small_sum, gain_sum,
    zx_all, rawg_all, dp_ref, buf, d_hidden, wide, d_left, entered, left, sums,
    normed_all, g_all, c_all, d_all, conv_x, small_x, spread_ref, *rest,
):
    step_at = pl.program_id(0)
    size = u_ref.shape[0]
    half = normed_all.shape[1] // 2
    count = zx_all.shape[0] // size
    names = (("loc", "rc", "ry", "rx", "rz", "out"), ("rc", "ry", "rx", "rz", "out"))
    sources = (
        (outg_hbm, out_sum, names[0]), ((gate0_hbm, gate1_hbm), gate_sum, names[0]),
        (conv_x, conv_sum, names[1]), (small_x, small_sum, names[1]),
    )
    bufs, at = [], 0
    for src, dst, held in sources:
        bufs.append(dict(zip(held, rest[at : at + len(held)]), src=src, dst=dst))
        at += len(held)
    load_sem = rest[-1]
    work = Reduction(plan, m, bufs, rest[at : at + 5])
    gains = (rest[at + 5 : at + 13], rest[at + 13 : at + 17])
    loads = [
        pltpu.make_async_copy(src, dst, load_sem.at[i])
        for i, (src, dst) in enumerate(
            ((normed_hbm, normed_all), (g_hbm, g_all), (c_hbm, c_all), (d_hbm, d_all))
        )
    ]

    conv_chunks = [k for k in range(len(plan)) if plan[k][0] == 2]
    small_chunks = [k for k in range(len(plan)) if plan[k][0] == 3]

    def tick(t):
        for k in range(len(plan)):
            if plan[k][0] < 2 and 0 <= t - begin[k] < 8:
                work.stage(k, t - begin[k])

    def slot(q):
        tick(blocks + q)
        for c, k in enumerate(conv_chunks):
            if 2 <= q + 1 - c < 8:
                work.stage(k, q + 1 - c)
        for k in small_chunks:
            if 2 <= q < 10:
                work.stage(k, q - 2)
        gain_hop(q - count)

    def gain_hop(hop):
        (gx, gc, gy, ga, gr, gb, gz, gsum), (sent, got, z_sent, z_got) = gains
        me = work.s

        def send(i, src, dst, peer):
            return pltpu.make_async_remote_copy(
                src, dst, sent.at[i], got.at[i], device_id=peer, device_id_type=MESH
            )

        hops = [
            [send(0, gx, gc, work.c_peer)], [send(1, gy.at[1 - me], gr.at[0], work.y_peer)],
            [send(2, ga, gr.at[1], work.x_peer)],
            [
                pltpu.make_async_remote_copy(
                    gb, gz.at[d - 1], z_sent.at[d - 1], z_got.at[d - 1], device_id=work.z_peer(d),
                    device_id_type=MESH,
                )
                for d in range(1, m)
            ],
        ]
        give = pltpu.make_async_copy(gsum, gain_sum, sent.at[3])
        if 0 < hop < 5:
            for copy in hops[hop - 1]:
                copy.wait_recv()
        if hop == 1:
            gy[...] = gx[...] + gc[...]
        elif hop == 2:
            ga[...] = gy[me] + gr[0]
        elif hop == 3:
            gb[...] = ga[...] + gr[1]
        elif hop == 4:
            result = gb[...]
            for d in range(1, m):
                result = result + gz[d - 1]
            gsum[...] = result
            give.start()
        elif hop == 5:
            for copy in hops[0] + hops[1] + hops[2] + hops[3]:
                copy.wait_send()
            give.wait()
        if 0 <= hop < 4:
            for copy in hops[hop]:
                copy.start()

    @pl.when(step_at == 0)
    def _():
        meet(work.peers())
        fill_spread(spread_ref)
        buf[BLOCK:, :] = jnp.zeros((8, XBC), f32)
        d_hidden[...] = jnp.zeros_like(d_hidden)
        dp_ref[...] = jnp.zeros_like(dp_ref)
        dp_ref[:, 44:50, :] = dgate_ref[:, :6, :]
        gains[0][0][...] = jnp.zeros_like(gains[0][0])

    for t in range(blocks):
        @pl.when(step_at == t)
        def _():
            tick(t)
            if t == 0:
                for load in loads:
                    load.start()

    @pl.when(step_at < blocks)
    def _():
        here = pl.ds(pl.multiple_of((blocks - 1 - step_at) * BLOCK, BLOCK), BLOCK)
        scan_back_step(
            here, aux_ref, p_ref, spread_ref, ci_ref, conv_ref, raw_ref, run_ref, y_ref, dy_ref, state_ref,
            zx_all, rawg_all, dp_ref, buf, d_hidden, wide, d_left, entered, left, sums,
        )

    for j in range(count):
        @pl.when(step_at == blocks + j)
        def _():
            if j == 0:
                for load in loads:
                    load.wait()
                if conv_x.shape[1] > XBC:
                    conv_x[:, XBC:] = jnp.zeros((2, conv_x.shape[1] - XBC, half), bf16)
                normed = normed_all[...]
                step_grad = mm(jnp.transpose(rawg_all[...])[:HEADS], normed)
                if small_x.shape[1] > LANES:
                    small_x[:, LANES:] = jnp.zeros((2, small_x.shape[1] - LANES, LANES), f32)
                for i in range(2):
                    for piece in range(half // LANES):
                        at = i * half + piece * LANES
                        row = 56 + piece * HEADS
                        small_x[i, row : row + HEADS, :] = step_grad[:, at : at + LANES]
                small_x[:, :56, :] = dp_ref[...]
                tick(blocks)
                for c, k in enumerate(conv_chunks):
                    _, start, rows = plan[k]
                    for at in range(start, min(start + rows, XBC), 256):
                        turned = jnp.transpose(zx_all[:, at : at + 256])
                        grad = mm(turned, normed).astype(bf16)
                        for i in range(2):
                            conv_x[i, at : at + 256, :] = grad[:, i * half : (i + 1) * half]
                    work.stage(k, 0)
                    if c > 0:
                        work.stage(conv_chunks[c - 1], 1)
                work.stage(conv_chunks[-1], 1)
            here = pl.ds(j * size, size)
            zg, zc, rg = zg_ref[...], zx_all[here, :], rawg_all[here, :HEADS]
            grad = jnp.concatenate(
                [mm(zg, g_all[i]) + mm(zc, c_all[i]) + mm(rg, d_all[i].astype(bf16)) for i in range(2)], axis=1
            )
            p = p_ref[...].astype(f32)
            u = u_ref[...].astype(f32)
            inv = lax.rsqrt(jnp.mean(u * u, axis=-1, keepdims=True) + eps)
            gain_part = total(grad * u * inv)
            for i in range(2):
                for piece in range(half // LANES):
                    at = i * half + piece * LANES
                    gains[0][0][i, piece : piece + 1, :] += gain_part[:, at : at + LANES]
            lifted = grad * gain_row(p)
            mean_u = jnp.mean(lifted * u, axis=-1, keepdims=True)
            ingrad_ref[...] = (
                g_ref[...].astype(f32) + inv * lifted - u * (inv * inv * inv * mean_u)
            ).astype(bf16)
            if j < count - 1:
                slot(j + 1)
            else:
                for q in range(count, max(count + 6, len(conv_chunks) + 6, 10, max(begin) + 8 - blocks)):
                    slot(q)
                work.finish()


def full(a):
    return pl.BlockSpec(a.shape, lambda i: (0,) * a.ndim, pipeline_mode=pl.Buffered(1))


def compute_params(mib=56):
    return pltpu.CompilerParams(
        dimension_semantics=("arbitrary",), vmem_limit_bytes=mib * 1024 * 1024
    )


def rows_of(size, cols, order):
    return pl.BlockSpec((size, cols), lambda i: (order(i), 0))


shape = jax.ShapeDtypeStruct
fwd = lambda i: i


def acc(rows):
    return pl.BlockSpec((2, rows, LANES), lambda i: (0, 0, 0))


def front(layer_in, seg, w_t, w_out, step_t, pack):
    tokens, width = layer_in.shape
    blocks = tokens // BLOCK
    half = width // 2
    rows = lambda cols: rows_of(BLOCK, cols, fwd)
    far_spec = pl.BlockSpec(memory_space=pl.ANY)
    pieces = ((XBC // 16, 4), (INNER // 8, 2), (w_out.shape[0] // 8, 2))
    n = sum(count for _, count in pieces)
    dma, vm = pltpu.SemaphoreType.DMA, pltpu.VMEM
    return pl.pallas_call(
        functools.partial(front_kernel, pieces, blocks),
        grid=(blocks,),
        in_specs=[rows(width), full(seg)] + [far_spec] * 4,
        out_specs=[
            rows(width), rows(XBC), rows(XBC), rows(LANES), rows(LANES), rows(INNER),
            pl.BlockSpec((1, STATE, INNER), lambda i: (i, 0, 0)), pl.BlockSpec((1, 16, BLOCK), lambda i: (i, 0, 0)),
        ]
        + [far_spec] * 5,
        out_shape=[
            shape((tokens, width), bf16), shape((tokens, XBC), bf16), shape((tokens, XBC), f32),
            shape((tokens, LANES), f32), shape((tokens, LANES), f32), shape((tokens, INNER), f32),
            shape((blocks, STATE, INNER), bf16), shape((blocks, 16, BLOCK), f32),
            shape((2, XBC, half), bf16), shape((2, INNER, half), bf16), shape((2,) + w_out.shape, bf16),
            shape((2,) + step_t.shape, f32), shape((2,) + pack.shape, f32),
        ],
        scratch_shapes=[
            vm((BLOCK + 8, XBC), f32), vm((STATE, INNER), f32), vm((3 * BLOCK + 8, INNER), f32),
            vm((BLOCK, INNER), f32), vm((2 * LANES, INNER), bf16),
            vm((2, XBC, half), bf16), vm((2,) + step_t.shape, f32), vm((2,) + pack.shape, f32),
            vm((INNER, half), bf16), vm(w_out.shape, bf16), vm((blocks, 16, BLOCK), f32),
            dma((10,)), dma((2, 2)), dma((4, n)), dma((4, n)),
        ],
        compiler_params=pltpu.CompilerParams(
            dimension_semantics=("arbitrary",), vmem_limit_bytes=56 * 1024 * 1024, collective_id=0,
            has_side_effects=True,
        ),
        cost_estimate=pl.CostEstimate(
            flops=2 * tokens * width * XBC * 4, bytes_accessed=30_000_000, transcendentals=tokens * 5000
        ),
        name="front",
    )(layer_in, seg, w_t, w_out, step_t, pack)


def gate_both(layer_in, normed, cotangent, y, g_all, o_all, pack):
    tokens, width = layer_in.shape
    size = 256
    rows = lambda cols: rows_of(size, cols, fwd)
    return pl.pallas_call(
        k2_kernel,
        grid=(tokens // size,),
        in_specs=[
            rows(width), rows(width), rows(width), rows(INNER), full(g_all), full(o_all), full(pack),
        ],
        out_specs=[rows(width), rows(INNER), rows(INNER), rows(INNER), acc(8)],
        out_shape=[
            shape((tokens, width), bf16), shape((tokens, INNER), bf16), shape((tokens, INNER), f32),
            shape((tokens, INNER), bf16), shape((2, 8, LANES), f32),
        ],
        scratch_shapes=[pltpu.VMEM((size, INNER), f32)] * 4,
        compiler_params=compute_params(),
        cost_estimate=pl.CostEstimate(
            flops=2 * tokens * width * INNER * 4, bytes_accessed=30_000_000, transcendentals=tokens * 5000
        ),
        name="gate_both",
    )(layer_in, normed, cotangent, y, g_all, o_all, pack)


def backward(
    layer_in, cotangent, aux, pack, ci, conv, raw, running, y, dy, states, zx_gate, d_gate, normed,
    g_all, c_all, d_all, out_grad, gate_grads,
):
    tokens, width = layer_in.shape
    blocks = tokens // BLOCK
    size = 256
    late = tokens // size
    half = width // 2
    m = lax.axis_size("rep") // 4

    def padded(rows, kind):
        unit = (16 if kind == bf16 else 8) * 4 * m
        return -(-rows // unit) * unit

    arrays = (
        (padded(out_grad.shape[1], bf16), width, bf16, 3, True), (padded(INNER, bf16), half, bf16, 3, True),
        (padded(XBC, bf16), half, bf16, late, False), (padded(LANES, f32), LANES, f32, 1, False),
    )
    plan, begin = [], []
    first = (0, 3, blocks, blocks)
    for which, (n, _, kind, pieces, _) in enumerate(arrays):
        units = n // ((16 if kind == bf16 else 8) * 4 * m)
        pieces = min(pieces, units)
        edges = [-(-units * i // pieces) * (n // units) for i in range(pieces + 1)]
        for i in range(pieces):
            plan.append((which, edges[i], edges[i + 1] - edges[i]))
            begin.append(first[which] + i if which < 2 else 0)
    grow = lambda a, n: jnp.pad(a, ((0, 0), (0, n - a.shape[1]), (0, 0)))
    out_grad = grow(out_grad, arrays[0][0])
    gate_grads = [grow(a[None], arrays[1][0])[0] for a in gate_grads]
    scratch = []
    for n, c, kind, _, far in arrays:
        if far:
            scratch.append(pltpu.VMEM((2, n // 2, c), kind))
        scratch += [
            pltpu.VMEM((2, n // 2, c), kind), pltpu.VMEM((n // 2, c), kind), pltpu.VMEM((n // 4, c), kind),
            pltpu.VMEM((max(m - 1, 1), n // (4 * m), c), kind), pltpu.VMEM((n, c), kind),
        ]
    chunks = len(plan)
    dma = pltpu.SemaphoreType.DMA
    back = lambda i: jnp.maximum(blocks - 1 - i, 0)
    row = lambda i: jnp.maximum(i - blocks, 0)
    rows = lambda cols: rows_of(BLOCK, cols, back)
    late_rows = lambda cols: rows_of(size, cols, row)
    far_spec = pl.BlockSpec(memory_space=pl.ANY)
    vm = pltpu.VMEM
    return pl.pallas_call(
        functools.partial(back_kernel, tuple(plan), tuple(begin), m, blocks),
        grid=(blocks + late,),
        in_specs=[
            pl.BlockSpec((1, 16, BLOCK), lambda i: (back(i), 0, 0)), full(pack),
            rows(XBC), rows(XBC), rows(LANES), rows(LANES), rows(INNER), rows(INNER),
            pl.BlockSpec((1, STATE, INNER), lambda i: (back(i), 0, 0)),
            late_rows(width), late_rows(width), late_rows(INNER), full(d_gate),
        ]
        + [far_spec] * 7,
        out_specs=[late_rows(width)] + [far_spec] * 5,
        out_shape=[shape((tokens, width), bf16)] + [shape((n, c), kind) for n, c, kind, _, _ in arrays]
        + [shape((8, LANES), f32)],
        scratch_shapes=[
            vm((tokens, XBC), bf16), vm((tokens, LANES), bf16), vm((2, 56, LANES), f32),
            vm((BLOCK + 8, XBC), f32), vm((STATE, INNER), f32), vm((3 * BLOCK + 8, INNER), f32),
            vm((BLOCK, INNER), f32), vm((BLOCK, INNER), bf16), vm((BLOCK, INNER), bf16),
            vm((4 * BLOCK + 32, INNER), bf16),
            vm(normed.shape, bf16), vm(g_all.shape, bf16), vm(c_all.shape, bf16), vm(d_all.shape, f32),
            vm((2, arrays[2][0], half), bf16), vm((2, arrays[3][0], LANES), f32),
            vm((2 * LANES, INNER), bf16),
        ]
        + scratch
        + [
            dma((6, chunks)), dma((6, chunks)), dma((2, chunks, max(m - 1, 1))),
            dma((2, chunks, max(m - 1, 1))), dma((3, chunks)),
            vm((2, 8, LANES), f32), vm((2, 8, LANES), f32), vm((2, 8, LANES), f32), vm((8, LANES), f32),
            vm((2, 8, LANES), f32), vm((8, LANES), f32), vm((max(m - 1, 1), 8, LANES), f32), vm((8, LANES), f32),
            dma((4,)), dma((3,)), dma((max(m - 1, 1),)), dma((max(m - 1, 1),)), dma((4,)),
        ],
        compiler_params=pltpu.CompilerParams(
            dimension_semantics=("arbitrary",), vmem_limit_bytes=62 * 1024 * 1024, collective_id=1,
            has_side_effects=True,
        ),
        cost_estimate=pl.CostEstimate(
            flops=2 * tokens * 768 * XBC * 8, bytes_accessed=40_000_000, transcendentals=tokens * 5000
        ),
        name="backward_reduce",
    )(aux, pack, ci, conv, raw, running, y, dy, states, layer_in, cotangent, zx_gate, d_gate,
      normed, g_all, c_all, d_all, out_grad, *gate_grads)


def pack_rows(norm_gain, conv_weight, conv_bias, dt_bias, a_log, skip_gain, gate_gain):
    pieces = (norm_gain, conv_weight.reshape(-1), conv_bias, gate_gain, dt_bias, a_log, skip_gain)
    size, at, flat = 48 * LANES, 0, None
    for v in pieces:
        wide = jnp.pad(v.astype(f32), (at, size - at - v.size))
        flat = wide if flat is None else flat + wide
        at += -(-v.size // LANES) * LANES
    return flat.reshape(-1, LANES)


def body(
    layer_in, segment_ids, cotangent, norm_gain, in_weight, conv_weight, conv_bias, dt_bias, a_log,
    skip_gain, gate_gain, out_weight,
):
    width = layer_in.shape[1]
    w_t = in_weight.T
    pack = pack_rows(norm_gain, conv_weight, conv_bias, dt_bias, a_log, skip_gain, gate_gain)
    step_t = w_t[WIDE:].astype(f32)
    normed, ci, conv, raw, running, y, states, aux, c_all, g_all, o_all, d_all, p_all = front(
        layer_in, segment_ids.reshape(-1, LANES), w_t, out_weight, step_t, pack
    )
    layer_out, mixed, dy, zx_gate, d_gate = gate_both(layer_in, normed, cotangent, y, g_all, o_all, p_all)
    nt = ((0,), (0,))
    half = width // 2
    by_half = lambda a: [mm(a, normed[:, i * half : (i + 1) * half], nt).astype(bf16) for i in range(2)]
    out_grad = mm(mixed, cotangent, nt).astype(bf16).reshape(2, -1, width)
    gate_grads = by_half(zx_gate)
    input_grad, out_sum, gate_sum, conv_sum, small_sum, gain_sum = backward(
        layer_in, cotangent, aux, p_all, ci, conv, raw, running, y, dy, states, zx_gate, d_gate,
        normed, g_all, c_all, d_all, out_grad, gate_grads,
    )
    factor = 1.0 / (lax.axis_size("shard") * lax.axis_size("rep"))
    small_sum = small_sum * factor
    pieces = half // LANES
    step_sum = small_sum[56 : 56 + pieces * HEADS].reshape(pieces, HEADS, LANES).transpose(1, 0, 2).reshape(HEADS, half)
    in_weight_grad = jnp.concatenate(
        [gate_sum[:INNER].astype(f32) * factor, conv_sum[:XBC].astype(f32) * factor, step_sum], axis=0
    ).T
    own = dt_bias.size
    head = lambda k: lax.dynamic_slice(small_sum[50 + k], (lax.axis_index("shard") * own,), (own,))
    return (
        layer_out, input_grad, (gain_sum[:3] * factor).reshape(norm_gain.shape), in_weight_grad,
        small_sum[3:31].reshape(conv_weight.shape), small_sum[31:38].reshape(conv_bias.shape),
        head(0), head(1), small_sum[38:44].reshape(own, HEADDIM).sum(axis=1),
        small_sum[44:50].reshape(gate_gain.shape), out_sum[: out_weight.shape[0]].astype(f32) * factor,
    )


def solution(mesh):
    both, shard = P(("shard", "rep"), None), P("shard")
    in_specs = (
        both, both, both, shard, P("shard", None), P(None, "shard"), shard, shard, shard, shard, shard,
        P("shard", None),
    )
    out_specs = (
        both, both, shard, P("shard", None), P(None, "shard"), shard, shard, shard, shard, shard,
        P("shard", None),
    )
    return jax.shard_map(body, mesh=mesh, in_specs=in_specs, out_specs=out_specs, check_vma=False)
```
